768 devices in a mesh: tile: 32 (over x, z_lo, core), spec: 24 (over y, z_hi).
Axes of the slice: x: 4, y: 8, z: 12 (z_hi: 3, z_lo: 4; z = z_hi * 4 + z_lo), core: 2. Of those that a mesh axis runs over, the one named last changes fastest.
Arguments:
- concentrations: float32 [192, 12288, 256], P('spec', 'tile'), may hold values from 0.1 to 4
- courant: float32 [12288, 256], P('tile'), may hold values from 0.05 to 0.95
- first_weight: bfloat16 [192, 512], replicated, may hold values from -0.4375 to 0.4375
- middle_weight: bfloat16 [512, 512], replicated, may hold values from -0.25 to 0.25
- last_weight: bfloat16 [512, 192], replicated, may hold values from -0.25 to 0.25
- active_blocks: int32 [32, 24, 16], P('tile', 'spec'), may hold values from 0 to 32, as said below
- dest_tile: int32 [32, 24, 16], P('tile', 'spec'), may hold values from 0 to 31, as said below
Outputs:
- chemistry_out: bfloat16 [192, 3145728], P(None, ('tile', 'spec'))
- load_share: float32 [32, 24], P('tile', 'spec')
The draws below stay inside these ranges and needn't reach their ends.
Inputs may be any that keep to these rules, and one draw needn't show every extreme that they name: `active_blocks`: each device's entries name distinct blocks of its own 32; the value 32 marks an empty slot. `dest_tile`: A listed block's tile lies within 2 tiles of its home tile along the periodic order of tiles; an empty slot names the home tile. At most 2 blocks of one device name one other tile, and at most 8 listed blocks over all devices of one spec index name one tile; both bounds are reached in every draw.
All inputs are finite; a program needn't handle non-finite values.
Results may differ from the reference program's by a relative error of at most 0.0035.
Values may be sent and summed in bfloat16 or wider, within the bound.
A program may use at most 32 MiB of HBM per device.

```python
import math
import jax
import jax.numpy as jnp
from jax import lax

HID = 512
BLK = 128
NB = 32
RECV = 8
CAP = 2
NBR = 2
ACT_MAX = 16
SPECIES = 192
NYL = 256
NX = 12288
CELLS = 3145728
N_TILE = 32
N_SPEC = 24


def plan_lists(key):
    base_key = jax.random.fold_in(key, 11)
    subkeys = jax.random.split(base_key, 6)
    tile_ids = jnp.arange(N_TILE, dtype=jnp.int32)[:, None]
    anchor = jax.random.randint(subkeys[0], (1, N_SPEC), 0, N_TILE)
    signed = (tile_ids - anchor + N_TILE // 2) % N_TILE - N_TILE // 2
    random_toss = jax.random.randint(subkeys[1], (N_TILE, N_SPEC), 0, 2)
    daytime = jnp.where(signed == 0, 1, jnp.where(jnp.abs(signed) <= NBR, 0, random_toss))
    is_anchor = (signed == 0).astype(jnp.int32)
    distances = [step_by for step_by in range(1, NBR + 1)] + [-step_by for step_by in range(1, NBR + 1)]
    take_list = []
    for number, distance in enumerate(distances):
        source_day = jnp.roll(daytime, distance, axis=0)
        source_anchor = jnp.roll(is_anchor, distance, axis=0)
        amount = jax.random.randint(jax.random.fold_in(subkeys[2], number), (N_TILE, N_SPEC), 1, CAP + 1)
        amount = jnp.where(source_anchor == 1, CAP, amount)
        take_list.append(jnp.where((daytime == 0) & (source_day == 1), amount, 0))
    intake = sum(take_list)
    spare_slot = jax.random.randint(subkeys[3], (N_TILE, N_SPEC), 0, 2)
    own_count = jnp.where(daytime == 1, RECV, jnp.maximum(RECV - intake - spare_slot, 0))
    sent_counts = [jnp.roll(taken_count, -distance, axis=0) for taken_count, distance in zip(take_list, distances)]
    counts = jnp.stack([own_count] + sent_counts, axis=-1)
    bounds = jnp.cumsum(counts, axis=-1)
    slot_ids = jnp.arange(ACT_MAX, dtype=jnp.int32)
    category = jnp.sum((slot_ids[None, None, :, None] >= bounds[:, :, None, :]).astype(jnp.int32), axis=-1)
    offset_table = jnp.array([0] + distances + [0], dtype=jnp.int32)
    shifts = offset_table[category]
    is_valid = slot_ids[None, None, :] < bounds[:, :, -1:]
    scores = jax.random.randint(subkeys[4], (N_TILE, N_SPEC, NB), 0, 1 << 20) * NB + jnp.arange(NB, dtype=jnp.int32)
    ranking = jnp.argsort(scores, axis=-1)[..., :ACT_MAX]
    blocks = jnp.where(is_valid, ranking, NB)
    targets = (tile_ids[:, :, None] + shifts) % N_TILE
    species_blending = jax.random.randint(subkeys[5], (N_TILE, N_SPEC, ACT_MAX), 0, 1 << 20) * ACT_MAX + slot_ids
    shuffle_order = jnp.argsort(species_blending, axis=-1)
    blocks = jnp.take_along_axis(blocks, shuffle_order, axis=-1)
    targets = jnp.take_along_axis(targets, shuffle_order, axis=-1)
    return (blocks.astype(jnp.int32), targets.astype(jnp.int32))


def draw_active_blocks(key, part):
    return plan_lists(key)[0]


def draw_dest_tile(key, part):
    return plan_lists(key)[1]


def steps_of(rng, dims, shards, low, high):
    level, own = 1.0, jax.random.fold_in(rng, 6)
    for axis_at, shards_of in shards:
        steps = jnp.exp(jax.random.uniform(jax.random.fold_in(own, axis_at), (shards_of,), jnp.float32, low / len(shards), high / len(shards)))
        level = level * jnp.repeat(steps, dims[axis_at] // shards_of).reshape([-1 if axis == axis_at else 1 for axis in range(len(dims))])
    return level


def centred(rng, shape, width, bound, held_as=jnp.bfloat16):
    return jnp.clip(width * jax.random.normal(rng, shape, jnp.float32), -bound, bound).astype(held_as)


def setup_inputs(seed: int = 0) -> dict:
    keys = jax.random.split(jax.random.key(seed), 8)
    concentrations = jnp.clip(jnp.exp(math.log(4.0) - 3.6888794 * jax.random.uniform(keys[0], (SPECIES, NX, NYL), jnp.float32) ** steps_of(keys[0], (SPECIES, NX, NYL), ((0, 24), (1, 32)), -0.2, 0.2)), 0.1, 4.0)
    courant = jnp.clip(0.05 + 0.9 * jax.random.uniform(keys[1], (NX, NYL), jnp.float32) ** steps_of(keys[1], (NX, NYL), ((0, 32),), -0.2, 0.2), 0.05, 0.95)
    first_weight = centred(keys[2], (SPECIES, HID), SPECIES ** -0.5, 0.4375)
    middle_weight = centred(keys[3], (HID, HID), HID ** -0.5, 0.25)
    last_weight = centred(keys[4], (HID, SPECIES), HID ** -0.5, 0.25)
    active_blocks = draw_active_blocks(jax.random.fold_in(keys[7], 71), 0)
    dest_tile = draw_dest_tile(jax.random.fold_in(keys[7], 71), 0)
    return dict(concentrations=concentrations, courant=courant, first_weight=first_weight, middle_weight=middle_weight, last_weight=last_weight, active_blocks=active_blocks, dest_tile=dest_tile)


def sweep_once(values, courant):
    left_diff = values - jnp.roll(values, 1, axis=0)
    right_diff = jnp.roll(values, -1, axis=0) - values
    slopes = jnp.where(left_diff * right_diff > 0, jnp.sign(left_diff) * jnp.minimum(jnp.abs(left_diff), jnp.abs(right_diff)), 0.0)
    fluxes = courant * (values + 0.5 * (1.0 - courant) * slopes)
    return values - fluxes + jnp.roll(fluxes, 1, axis=0)


def surrogate(inputs, first_weight, middle_weight, last_weight):
    first_layer = jax.nn.silu(jnp.dot(first_weight.T, inputs, preferred_element_type=jnp.float32)).astype(jnp.bfloat16)
    second = jax.nn.silu(jnp.dot(middle_weight.T, first_layer, preferred_element_type=jnp.float32)).astype(jnp.bfloat16)
    change = jnp.dot(last_weight.T, second, preferred_element_type=jnp.float32)
    return (inputs.astype(jnp.float32) + change).astype(jnp.bfloat16)


def reference(concentrations, courant, first_weight, middle_weight, last_weight, active_blocks, dest_tile):
    def advect_species(values):
        for repeat in range(2):
            values = sweep_once(values, courant)
        return values.astype(jnp.bfloat16)

    advected = lax.map(advect_species, concentrations)
    devices_all = N_TILE * N_SPEC
    cell_table = advected.reshape(SPECIES, devices_all, NB, BLK).transpose(1, 2, 0, 3)
    list_table = active_blocks.reshape(devices_all, ACT_MAX)

    def chem_device(operands):
        blocks_dev, listing = operands
        safe_index = jnp.minimum(listing, NB - 1).astype(jnp.int32)
        picked = blocks_dev[safe_index].transpose(1, 0, 2).reshape(SPECIES, ACT_MAX * BLK)
        refreshed_state = surrogate(picked, first_weight, middle_weight, last_weight)
        refreshed_state = refreshed_state.reshape(SPECIES, ACT_MAX, BLK).transpose(1, 0, 2)
        return blocks_dev.at[listing.astype(jnp.int32)].set(refreshed_state, mode="drop")

    new_cells = lax.map(chem_device, (cell_table, list_table))
    chemistry_out = new_cells.transpose(2, 0, 1, 3).reshape(SPECIES, CELLS)
    hit_table = (dest_tile[..., None] == jnp.arange(N_TILE, dtype=jnp.int32)) & (active_blocks < NB)[..., None]
    load_share = jnp.sum(hit_table.astype(jnp.float32), axis=(0, 2)).T / RECV
    return chemistry_out, load_share
```

```python
import functools

import jax
import jax.numpy as jnp
from jax import lax
from jax.experimental import pallas as pl
from jax.experimental.pallas import tpu as pltpu
from jax.sharding import PartitionSpec as P

BLK = 128
RECV = 8
NBR = 2
GROUPS = 8
PAD = 8
MESH = pl.DeviceIdType.MESH
F32 = jnp.float32
BF16 = jnp.bfloat16


def minmod(left, right):
    return jnp.maximum(jnp.minimum(left, right), 0.0) + jnp.minimum(jnp.maximum(left, right), 0.0)


def fused_silu(half):
    return (half + half * jnp.tanh(half)).astype(BF16)


def kernel(
    n_tile, n_spec, n_z, n_group,
    conc, courant, w1_hbm, w2_hbm, w3_hbm, active, dest,
    out, share,
    field, rate, half_rest, field_in, rate_in, send, recv, w1, w2, w1_t, w2_t, w3_t, counts, counts_in,
    load_sem, weight_sem, halo_send, halo_recv, count_send, count_recv, send_sem, recv_sem, own_sem,
):
    tile = lax.axis_index("tile")
    me = lax.axis_index("spec")
    my_y, my_z = me // n_z, me % n_z
    n_y = n_spec // n_z
    rows = conc.shape[1]
    deep = rows + 2 * PAD
    share_rows = rows // n_spec
    width = conc.shape[2]
    halves = width // BLK
    per_group = share_rows // n_group
    up, down = (tile + 1) % n_tile, (tile + n_tile - 1) % n_tile

    def partner(k):
        return ((my_y + k) % n_y) * n_z + (my_z + k) % n_z

    species = conc.shape[0]

    def load(s, carry):
        for c in range(halves):
            pltpu.make_async_copy(
                conc.at[s, :, pl.ds(c * BLK, BLK)], field.at[c, pl.ds(pl.multiple_of(s * deep + PAD, PAD), rows), :], load_sem.at[c]
            ).start()
        return carry

    lax.fori_loop(0, species, load, 0)
    loads = []
    for c in range(halves):
        loads.append(pltpu.make_async_copy(
            courant.at[:, pl.ds(c * BLK, BLK)], rate.at[c, pl.ds(PAD, rows), :], load_sem.at[halves + c]))
        loads[-1].start()
        whole = field.at[c, pl.ds(0, species * rows), :]
        loads.append(pltpu.make_async_copy(whole, whole, load_sem.at[c]))
    weights = [
        pltpu.make_async_copy(w1_hbm, w1, weight_sem.at[0]),
        pltpu.make_async_copy(w2_hbm, w2, weight_sem.at[1]),
        pltpu.make_async_copy(w3_hbm, w3_t, weight_sem.at[2]),
    ]
    for copy in weights:
        copy.start()

    barrier = pltpu.get_barrier_semaphore()

    def greet(k, carry):
        pl.semaphore_signal(barrier, inc=1, device_id={"spec": partner(k)}, device_id_type=MESH)
        return carry

    lax.fori_loop(1, n_spec, greet, 0)
    steps = [1, -1, 2, -2]
    for step in steps:
        pl.semaphore_signal(barrier, inc=1, device_id={"tile": (tile + step + n_tile) % n_tile}, device_id_type=MESH)

    named = [jnp.int32(0)] * 5
    for j in range(active.shape[0]):
        home = (dest[j] - tile + n_tile + n_tile // 2) % n_tile - n_tile // 2
        valid = active[j] < out.shape[1] // BLK
        for i, step in enumerate([0] + steps):
            named[i] = named[i] + jnp.where(valid & (home == step), 1, 0)
    for i in range(5):
        counts[i] = jnp.full(counts.shape[1:], named[i], jnp.int32)

    for copy in loads:
        copy.wait()
    for c in range(halves):
        half_rest[c, PAD : PAD + rows] = 0.5 * (1.0 - rate[c, PAD : PAD + rows])

    def advect(d):
        first = PAD + d * share_rows
        finished = []
        for c in range(halves):
            def value(i):
                return field[c, pl.ds(first + i, species, stride=deep), :]

            def rates(i):
                return rate[c, pl.ds(first + i, 1), :], half_rest[c, pl.ds(first + i, 1), :]

            def flux(i, mid, left, right):
                speed, rest = rates(i)
                return speed * (mid + rest * minmod(left, right))

            before, mid = value(-4), value(-3)
            left = mid - before
            flow, once = None, {}
            done = []
            previous, left2, flow2 = None, None, None
            for i in range(-3, share_rows + 1):
                after = value(i + 1)
                right = after - mid
                now = flux(i, mid, left, right)
                if flow is not None:
                    fresh = mid - now + flow
                    once[i] = fresh
                    if i - 1 in once:
                        right2 = fresh - once[i - 1]
                        if left2 is not None:
                            now2 = flux(i - 1, once[i - 1], left2, right2)
                            if flow2 is not None:
                                done.append(once[i - 1] - now2 + flow2)
                            flow2 = now2
                        left2 = right2
                flow, mid, left = now, after, right
            finished.append(done)
        for r in range(share_rows):
            both = jnp.concatenate([finished[c][r] for c in range(halves)], axis=1)
            spot = (r % per_group) * width
            send[d, r // per_group, :, spot : spot + width] = both.astype(BF16)

    def inner(d, carry):
        advect(d)
        return carry

    lax.fori_loop(1, n_spec - 1, inner, 0)

    pl.semaphore_wait(barrier, n_spec - 1 + len(steps))

    sides = [(rows - PAD, 0, up), (0, PAD + rows, down)]

    def send_halo(s, carry):
        for index, (origin, target, device) in enumerate(sides):
            for c in range(halves):
                pltpu.make_async_remote_copy(
                    conc.at[s, pl.ds(origin, PAD), pl.ds(c * BLK, BLK)],
                    field_in.at[index, c, pl.ds(pl.multiple_of(s * PAD, PAD), PAD), :],
                    halo_send.at[index], halo_recv.at[index], device_id={"tile": device}, device_id_type=MESH).start()
        return carry

    lax.fori_loop(0, species, send_halo, 0)
    halo = []
    for index, (origin, target, device) in enumerate(sides):
        whole = field_in.at[index]
        halo.append(pltpu.make_async_remote_copy(
            whole, whole, halo_send.at[index], halo_recv.at[index], device_id={"tile": device}, device_id_type=MESH))
        for c in range(halves):
            halo.append(pltpu.make_async_remote_copy(
                courant.at[pl.ds(origin, PAD), pl.ds(c * BLK, BLK)], rate_in.at[index, c],
                halo_send.at[2 + 2 * c + index], halo_recv.at[2 + 2 * c + index], device_id={"tile": device}, device_id_type=MESH))
            halo[-1].start()
    tallies = []
    for i, step in enumerate(steps):
        tallies.append(pltpu.make_async_remote_copy(
            counts.at[i + 1], counts_in.at[i], count_send.at[i], count_recv.at[i],
            device_id={"tile": (tile + step + n_tile) % n_tile}, device_id_type=MESH))
    for copy in tallies:
        copy.start()

    def message(d, g):
        return pltpu.make_async_remote_copy(
            send.at[d, g], recv.at[g, me], send_sem, recv_sem.at[g], device_id={"spec": d}, device_id_type=MESH)

    def first_group(k, carry):
        d = partner(k)

        @pl.when((d != 0) & (d != n_spec - 1))
        def _():
            message(d, 0).start()
        return carry

    lax.fori_loop(1, n_spec, first_group, 0)

    for copy in halo:
        copy.wait()
    for c in range(halves):
        for index, (_, target, _) in enumerate(sides):
            rate[c, target : target + PAD] = rate_in[index, c]
            for s in range(species):
                field[c, s * deep + target : s * deep + target + PAD] = field_in[index, c, s * PAD : (s + 1) * PAD]
            half_rest[c, target : target + PAD] = 0.5 * (1.0 - rate[c, target : target + PAD])

    def edge(e, carry):
        d = e * (n_spec - 1)
        advect(d)

        @pl.when(d != me)
        def _():
            message(d, 0).start()
        return carry

    lax.fori_loop(0, 2, edge, 0)

    def later(i, carry):
        g = i // (n_spec - 1)
        message(partner(i % (n_spec - 1) + 1), g).start()
        return carry

    lax.fori_loop(n_spec - 1, n_group * (n_spec - 1), later, 0)

    own = pltpu.make_async_copy(send.at[me], recv.at[:, me], own_sem)
    own.start()

    for copy in weights:
        copy.wait()
    w1_t[...] = (w1[...] * BF16(0.5)).T
    w2_t[...] = (w2[...] * BF16(0.5)).T
    own.wait()

    span = recv.shape[3]
    total = n_spec * species

    def integrate(g, carry):
        pltpu.make_async_remote_copy(
            recv.at[g, pl.ds(0, n_spec - 1)], recv.at[g, pl.ds(0, n_spec - 1)], send_sem, recv_sem.at[g],
            device_id={"spec": me}, device_id_type=MESH).wait_recv()
        x = recv[g].reshape(total, span)
        one = fused_silu(jnp.dot(w1_t[...], x, preferred_element_type=F32))
        two = fused_silu(jnp.dot(w2_t[...], one, preferred_element_type=F32))
        change = jnp.dot(w3_t[...], two, preferred_element_type=F32)
        fresh = (x.astype(F32) + change).astype(BF16)
        for b in range(span // BLK):
            block = g * (span // BLK) + b
            listed = jnp.int32(0)
            for j in range(active.shape[0]):
                listed = listed + jnp.where(active[j] == block, 1, 0)
            cols = slice(b * BLK, (b + 1) * BLK)
            chosen = jnp.where(jnp.full((total, BLK), listed, jnp.int32) > 0, fresh[:, cols].astype(F32), x[:, cols].astype(F32))
            out[:, pl.ds(pl.multiple_of(block * BLK, BLK), BLK)] = chosen.astype(BF16)
        return carry

    lax.fori_loop(0, n_group, integrate, 0)

    for copy in tallies:
        copy.wait()
    tally = counts[0] + counts_in[0] + counts_in[1] + counts_in[2] + counts_in[3]
    share[...] = tally[0:1, 0:1].astype(F32) / RECV

    pltpu.make_async_remote_copy(
        recv.at[:, pl.ds(0, n_spec - 1)], recv.at[:, pl.ds(0, n_spec - 1)], send_sem, own_sem,
        device_id={"spec": me}, device_id_type=MESH).wait_send()


def solution(mesh):
    n_tile, n_spec = mesh.shape["tile"], mesh.shape["spec"]

    def shards(conc, courant, w1, w2, w3, active, dest):
        species, rows, width = conc.shape
        hidden = w2.shape[0]
        halves = width // BLK
        total = n_spec * species
        cells = rows // n_spec * width
        span = cells // GROUPS
        deep = rows + 2 * PAD
        anywhere = pl.BlockSpec(memory_space=pl.ANY)
        scalars = pl.BlockSpec(memory_space=pltpu.SMEM)
        vector = pl.BlockSpec(memory_space=pltpu.VMEM)
        out, share = pl.pallas_call(
            functools.partial(kernel, n_tile, n_spec, 3, GROUPS),
            out_shape=(jax.ShapeDtypeStruct((total, cells), BF16), jax.ShapeDtypeStruct((1, 1), F32)),
            in_specs=[anywhere] * 5 + [scalars] * 2,
            out_specs=(vector, vector),
            scratch_shapes=[
                pltpu.VMEM((halves, species * deep, BLK), F32),
                pltpu.VMEM((halves, deep, BLK), F32),
                pltpu.VMEM((halves, deep, BLK), F32),
                pltpu.VMEM((2, halves, species * PAD, BLK), F32),
                pltpu.VMEM((2, halves, PAD, BLK), F32),
                pltpu.VMEM((n_spec, GROUPS, species, span), BF16),
                pltpu.VMEM((GROUPS, n_spec, species, span), BF16),
                pltpu.VMEM((total, hidden), BF16),
                pltpu.VMEM((hidden, hidden), BF16),
                pltpu.VMEM((hidden, total), BF16),
                pltpu.VMEM((hidden, hidden), BF16),
                pltpu.VMEM((total, hidden), BF16),
                pltpu.VMEM((5, 8, BLK), jnp.int32),
                pltpu.VMEM((4, 8, BLK), jnp.int32),
                pltpu.SemaphoreType.DMA((2 * halves,)),
                pltpu.SemaphoreType.DMA((3,)),
                pltpu.SemaphoreType.DMA((2 + 2 * halves,)),
                pltpu.SemaphoreType.DMA((2 + 2 * halves,)),
                pltpu.SemaphoreType.DMA((4,)),
                pltpu.SemaphoreType.DMA((4,)),
                pltpu.SemaphoreType.DMA,
                pltpu.SemaphoreType.DMA((GROUPS,)),
                pltpu.SemaphoreType.DMA,
            ],
            compiler_params=pltpu.CompilerParams(
                collective_id=0, has_side_effects=True, vmem_limit_bytes=60 * 1024 * 1024
            ),
            name="sweep_exchange_chemistry",
        )(conc, courant, w1, w2, w3.T, active.reshape(-1), dest.reshape(-1))
        return out, share

    in_specs = (
        P("spec", "tile", None),
        P("tile", None),
        P(),
        P(),
        P(),
        P("tile", "spec", None),
        P("tile", "spec", None),
    )
    out_specs = (P(None, ("tile", "spec")), P("tile", "spec"))
    return jax.shard_map(shards, mesh=mesh, in_specs=in_specs, out_specs=out_specs, check_vma=False)
```

```python
import functools

import jax
import jax.numpy as jnp
from jax import lax
from jax.experimental import pallas as pl
from jax.experimental.pallas import tpu as pltpu
from jax.sharding import PartitionSpec as P

BLK = 128
RECV = 8
NBR = 2
GROUPS = 8
PAD = 8
MESH = pl.DeviceIdType.MESH
F32 = jnp.float32
BF16 = jnp.bfloat16


def minmod(left, right):
    return jnp.maximum(jnp.minimum(left, right), 0.0) + jnp.minimum(jnp.maximum(left, right), 0.0)


def fused_silu(half):
    return (half + half * jnp.tanh(half)).astype(BF16)


def kernel(
    n_tile, n_spec, n_z, n_group,
    conc, courant, w1_hbm, w2_hbm, w3_hbm, active, dest,
    out, share,
    field, rate, half_rest, field_out, field_in, rate_in, send, recv, w1, w2, w1_t, w2_t, w3_t, counts, counts_in,
    load_sem, weight_sem, halo_send, halo_recv, count_send, count_recv, send_sem, recv_sem, own_sem, known,
):
    tile = lax.axis_index("tile")
    me = lax.axis_index("spec")
    my_y, my_z = me // n_z, me % n_z
    n_y = n_spec // n_z
    rows = conc.shape[1]
    deep = rows + 2 * PAD
    share_rows = rows // n_spec
    width = conc.shape[2]
    halves = width // BLK
    per_group = share_rows // n_group
    up, down = (tile + 1) % n_tile, (tile + n_tile - 1) % n_tile

    def partner(k):
        return ((my_y + k) % n_y) * n_z + (my_z + k) % n_z

    species = conc.shape[0]

    def load(s, carry):
        for c in range(halves):
            pltpu.make_async_copy(
                conc.at[s, :, pl.ds(c * BLK, BLK)], field.at[c, pl.ds(pl.multiple_of(s * deep + PAD, PAD), rows), :], load_sem.at[c]
            ).start()
        return carry

    lax.fori_loop(0, species, load, 0)
    loads = []
    for c in range(halves):
        loads.append(pltpu.make_async_copy(
            courant.at[:, pl.ds(c * BLK, BLK)], rate.at[c, pl.ds(PAD, rows), :], load_sem.at[halves + c]))
        loads[-1].start()
        whole = field.at[c, pl.ds(0, species * rows), :]
        loads.append(pltpu.make_async_copy(whole, whole, load_sem.at[c]))
    weights = [
        pltpu.make_async_copy(w1_hbm, w1, weight_sem.at[0]),
        pltpu.make_async_copy(w2_hbm, w2, weight_sem.at[1]),
        pltpu.make_async_copy(w3_hbm, w3_t, weight_sem.at[2]),
    ]
    for copy in weights:
        copy.start()

    barrier = pltpu.get_barrier_semaphore()

    def at(dy, dz):
        return ((my_y + dy + n_y) % n_y) * n_z + (my_z + dz) % n_z

    steps = [1, -1, 2, -2]
    column = list(range(1, n_z))
    for dz in column:
        pl.semaphore_signal(barrier, inc=1, device_id={"spec": at(0, dz)}, device_id_type=MESH)
    for dy in (1, -1):
        pl.semaphore_signal(barrier, inc=1, device_id={"spec": at(dy, 0)}, device_id_type=MESH)
    for step in steps:
        pl.semaphore_signal(barrier, inc=1, device_id={"tile": (tile + step + n_tile) % n_tile}, device_id_type=MESH)

    named = [jnp.int32(0)] * 5
    for j in range(active.shape[0]):
        home = (dest[j] - tile + n_tile + n_tile // 2) % n_tile - n_tile // 2
        valid = active[j] < out.shape[1] // BLK
        for i, step in enumerate([0] + steps):
            named[i] = named[i] + jnp.where(valid & (home == step), 1, 0)
    for i in range(5):
        counts[i] = jnp.full(counts.shape[1:], named[i], jnp.int32)

    for copy in loads:
        copy.wait()
    for c in range(halves):
        half_rest[c, PAD : PAD + rows] = 0.5 * (1.0 - rate[c, PAD : PAD + rows])

    sides = [(PAD + rows - 4, 4, 4, up), (PAD, PAD + rows, 2, down)]
    for index, (origin, _, thick, _) in enumerate(sides):
        for c in range(halves):
            for s in range(species):
                field_out[index, c, s * thick : (s + 1) * thick] = field[c, s * deep + origin : s * deep + origin + thick]

    def advect(d):
        first = PAD + d * share_rows
        finished = []
        for c in range(halves):
            def value(i):
                return field[c, pl.ds(first + i, species, stride=deep), :]

            def rates(i):
                return rate[c, pl.ds(first + i, 1), :], half_rest[c, pl.ds(first + i, 1), :]

            def flux(i, mid, left, right):
                speed, rest = rates(i)
                return speed * (mid + rest * minmod(left, right))

            before, mid = value(-4), value(-3)
            left = mid - before
            flow, once = None, {}
            done = []
            previous, left2, flow2 = None, None, None
            for i in range(-3, share_rows + 1):
                after = value(i + 1)
                right = after - mid
                now = flux(i, mid, left, right)
                if flow is not None:
                    fresh = mid - now + flow
                    once[i] = fresh
                    if i - 1 in once:
                        right2 = fresh - once[i - 1]
                        if left2 is not None:
                            now2 = flux(i - 1, once[i - 1], left2, right2)
                            if flow2 is not None:
                                done.append(once[i - 1] - now2 + flow2)
                            flow2 = now2
                        left2 = right2
                flow, mid, left = now, after, right
            finished.append(done)
        for r in range(share_rows):
            both = jnp.concatenate([finished[c][r] for c in range(halves)], axis=1)
            spot = (r % per_group) * width
            send[d, r // per_group, :, spot : spot + width] = both.astype(BF16)

    def inner(d, carry):
        advect(d)
        return carry

    lax.fori_loop(1, n_spec - 1, inner, 0)

    pl.semaphore_wait(barrier, len(column) + 2 + len(steps))

    def message(d, g):
        return pltpu.make_async_remote_copy(
            send.at[d, g], recv.at[g, me], send_sem, recv_sem.at[g], device_id={"spec": d}, device_id_type=MESH)

    def inside(d):
        return (d != 0) & (d != n_spec - 1)

    for dz in column:
        @pl.when(inside(at(0, dz)))
        def _(d=at(0, dz)):
            def every(g, carry):
                message(d, g).start()
                return carry

            lax.fori_loop(0, n_group, every, 0)

    halo = []
    for index, (_, _, thick, device) in enumerate(sides):
        for c in range(halves):
            halo.append(pltpu.make_async_remote_copy(
                field_out.at[index, c, pl.ds(0, species * thick)], field_in.at[index, c, pl.ds(0, species * thick)],
                halo_send.at[2 * c + index], halo_recv.at[2 * c + index], device_id={"tile": device}, device_id_type=MESH))
            halo.append(pltpu.make_async_remote_copy(
                rate.at[c, pl.ds(PAD + (rows - PAD if index == 0 else 0), PAD), :], rate_in.at[index, c],
                halo_send.at[4 + 2 * c + index], halo_recv.at[4 + 2 * c + index], device_id={"tile": device}, device_id_type=MESH))
    for copy in halo:
        copy.start()
    tallies = []
    for i, step in enumerate(steps):
        tallies.append(pltpu.make_async_remote_copy(
            counts.at[i + 1], counts_in.at[i], count_send.at[i], count_recv.at[i],
            device_id={"tile": (tile + step + n_tile) % n_tile}, device_id_type=MESH))
    for copy in tallies:
        copy.start()

    for reach in range(1, n_y // 2 + 1):
        for way, dy in enumerate((1, -1)):
            pl.semaphore_signal(known.at[reach - 1, way], inc=1, device_id={"spec": at(dy, 0)}, device_id_type=MESH)
        for way in range(2):
            pl.semaphore_wait(known.at[reach - 1, way], 1)
        for dy in sorted({reach, n_y - reach}):
            for dz in column + [0]:
                @pl.when(inside(at(dy, dz)))
                def _(d=at(dy, dz)):
                    message(d, 0).start()

    for copy in halo:
        copy.wait()
    for c in range(halves):
        for index, (_, target, thick, _) in enumerate(sides):
            base = index * (PAD + rows)
            rate[c, base : base + PAD] = rate_in[index, c]
            for s in range(species):
                field[c, s * deep + target : s * deep + target + thick] = field_in[index, c, s * thick : (s + 1) * thick]
            half_rest[c, base : base + PAD] = 0.5 * (1.0 - rate[c, base : base + PAD])

    def edge(e, carry):
        d = e * (n_spec - 1)
        advect(d)

        @pl.when(d != me)
        def _():
            message(d, 0).start()
        return carry

    lax.fori_loop(0, 2, edge, 0)

    def later(i, carry):
        g, k = i // (n_spec - 1), i % (n_spec - 1) + 1
        d = partner(k)

        @pl.when((k % n_y != 0) | (d == 0) | (d == n_spec - 1))
        def _():
            message(d, g).start()
        return carry

    lax.fori_loop(n_spec - 1, n_group * (n_spec - 1), later, 0)

    own = pltpu.make_async_copy(send.at[me], recv.at[:, me], own_sem)
    own.start()

    for copy in weights:
        copy.wait()
    w1_t[...] = (w1[...] * BF16(0.5)).T
    w2_t[...] = (w2[...] * BF16(0.5)).T
    own.wait()

    span = recv.shape[3]
    total = n_spec * species

    def integrate(g, carry):
        pltpu.make_async_remote_copy(
            recv.at[g, pl.ds(0, n_spec - 1)], recv.at[g, pl.ds(0, n_spec - 1)], send_sem, recv_sem.at[g],
            device_id={"spec": me}, device_id_type=MESH).wait_recv()
        x = recv[g].reshape(total, span)
        one = fused_silu(jnp.dot(w1_t[...], x, preferred_element_type=F32))
        two = fused_silu(jnp.dot(w2_t[...], one, preferred_element_type=F32))
        change = jnp.dot(w3_t[...], two, preferred_element_type=F32)
        fresh = (x.astype(F32) + change).astype(BF16)
        for b in range(span // BLK):
            block = g * (span // BLK) + b
            listed = jnp.int32(0)
            for j in range(active.shape[0]):
                listed = listed + jnp.where(active[j] == block, 1, 0)
            cols = slice(b * BLK, (b + 1) * BLK)
            chosen = jnp.where(jnp.full((total, BLK), listed, jnp.int32) > 0, fresh[:, cols].astype(F32), x[:, cols].astype(F32))
            out[:, pl.ds(pl.multiple_of(block * BLK, BLK), BLK)] = chosen.astype(BF16)
        return carry

    lax.fori_loop(0, n_group, integrate, 0)

    for copy in tallies:
        copy.wait()
    tally = counts[0] + counts_in[0] + counts_in[1] + counts_in[2] + counts_in[3]
    share[...] = tally[0:1, 0:1].astype(F32) / RECV

    pltpu.make_async_remote_copy(
        recv.at[:, pl.ds(0, n_spec - 1)], recv.at[:, pl.ds(0, n_spec - 1)], send_sem, own_sem,
        device_id={"spec": me}, device_id_type=MESH).wait_send()


def solution(mesh):
    n_tile, n_spec = mesh.shape["tile"], mesh.shape["spec"]

    def shards(conc, courant, w1, w2, w3, active, dest):
        species, rows, width = conc.shape
        hidden = w2.shape[0]
        halves = width // BLK
        total = n_spec * species
        cells = rows // n_spec * width
        span = cells // GROUPS
        deep = rows + 2 * PAD
        anywhere = pl.BlockSpec(memory_space=pl.ANY)
        scalars = pl.BlockSpec(memory_space=pltpu.SMEM)
        vector = pl.BlockSpec(memory_space=pltpu.VMEM)
        out, share = pl.pallas_call(
            functools.partial(kernel, n_tile, n_spec, 3, GROUPS),
            out_shape=(pltpu.VMEM((total, cells), BF16), jax.ShapeDtypeStruct((1, 1), F32)),
            in_specs=[anywhere] * 5 + [scalars] * 2,
            out_specs=(vector, vector),
            scratch_shapes=[
                pltpu.VMEM((halves, species * deep, BLK), F32),
                pltpu.VMEM((halves, deep, BLK), F32),
                pltpu.VMEM((halves, deep, BLK), F32),
                pltpu.VMEM((2, halves, species * 4, BLK), F32),
                pltpu.VMEM((2, halves, species * 4, BLK), F32),
                pltpu.VMEM((2, halves, PAD, BLK), F32),
                pltpu.VMEM((n_spec, GROUPS, species, span), BF16),
                pltpu.VMEM((GROUPS, n_spec, species, span), BF16),
                pltpu.VMEM((total, hidden), BF16),
                pltpu.VMEM((hidden, hidden), BF16),
                pltpu.VMEM((hidden, total), BF16),
                pltpu.VMEM((hidden, hidden), BF16),
                pltpu.VMEM((total, hidden), BF16),
                pltpu.VMEM((5, 8, BLK), jnp.int32),
                pltpu.VMEM((4, 8, BLK), jnp.int32),
                pltpu.SemaphoreType.DMA((2 * halves,)),
                pltpu.SemaphoreType.DMA((3,)),
                pltpu.SemaphoreType.DMA((4 * halves,)),
                pltpu.SemaphoreType.DMA((4 * halves,)),
                pltpu.SemaphoreType.DMA((4,)),
                pltpu.SemaphoreType.DMA((4,)),
                pltpu.SemaphoreType.DMA,
                pltpu.SemaphoreType.DMA((GROUPS,)),
                pltpu.SemaphoreType.DMA,
                pltpu.SemaphoreType.REGULAR((max(n_spec // 6, 1), 2)),
            ],
            compiler_params=pltpu.CompilerParams(
                collective_id=0, has_side_effects=True, vmem_limit_bytes=60 * 1024 * 1024
            ),
            name="sweep_exchange_chemistry",
        )(conc, courant, w1, w2, w3.T, active.reshape(-1), dest.reshape(-1))
        return out, share

    in_specs = (
        P("spec", "tile", None),
        P("tile", None),
        P(),
        P(),
        P(),
        P("tile", "spec", None),
        P("tile", "spec", None),
    )
    out_specs = (P(None, ("tile", "spec")), P("tile", "spec"))
    return jax.shard_map(shards, mesh=mesh, in_specs=in_specs, out_specs=out_specs, check_vma=False)
```

```python
import functools

import jax
import jax.numpy as jnp
from jax import lax
from jax.experimental import pallas as pl
from jax.experimental.pallas import tpu as pltpu
from jax.sharding import PartitionSpec as P

BLK = 128
RECV = 8
NBR = 2
GROUPS = 8
PAD = 8
MESH = pl.DeviceIdType.MESH
F32 = jnp.float32
BF16 = jnp.bfloat16


def minmod(left, right):
    return jnp.maximum(jnp.minimum(left, right), 0.0) + jnp.minimum(jnp.maximum(left, right), 0.0)


def fused_silu(half):
    return (half + half * jnp.tanh(half)).astype(BF16)


def kernel(
    n_tile, n_spec, n_z, n_group,
    conc, courant, w1_hbm, w2_hbm, w3_hbm, active, dest,
    out, share,
    field, rate, half_rest, field_out, field_in, rate_in, send, recv, w1, w2, w1_t, w2_t, w3_t, counts, counts_in,
    load_sem, weight_sem, halo_send, halo_recv, count_send, count_recv, send_sem, recv_sem, own_sem, known,
):
    tile = lax.axis_index("tile")
    me = lax.axis_index("spec")
    my_y, my_z = me // n_z, me % n_z
    n_y = n_spec // n_z
    rows = conc.shape[1]
    deep = rows + 2 * PAD
    share_rows = rows // n_spec
    width = conc.shape[2]
    halves = width // BLK
    per_group = share_rows // n_group
    up, down = (tile + 1) % n_tile, (tile + n_tile - 1) % n_tile

    def partner(k):
        return ((my_y + k) % n_y) * n_z + (my_z + k) % n_z

    species = conc.shape[0]

    def load(s, carry):
        for c in range(halves):
            pltpu.make_async_copy(
                conc.at[s, :, pl.ds(c * BLK, BLK)], field.at[c, pl.ds(pl.multiple_of(s * deep + PAD, PAD), rows), :], load_sem.at[c]
            ).start()
        return carry

    lax.fori_loop(0, species, load, 0)
    loads = []
    for c in range(halves):
        loads.append(pltpu.make_async_copy(
            courant.at[:, pl.ds(c * BLK, BLK)], rate.at[c, pl.ds(PAD, rows), :], load_sem.at[halves + c]))
        loads[-1].start()
        whole = field.at[c, pl.ds(0, species * rows), :]
        loads.append(pltpu.make_async_copy(whole, whole, load_sem.at[c]))
    weights = [
        pltpu.make_async_copy(w1_hbm, w1, weight_sem.at[0]),
        pltpu.make_async_copy(w2_hbm, w2, weight_sem.at[1]),
        pltpu.make_async_copy(w3_hbm, w3_t, weight_sem.at[2]),
    ]
    for copy in weights:
        copy.start()

    barrier = pltpu.get_barrier_semaphore()

    def at(dy, dz):
        return ((my_y + dy + n_y) % n_y) * n_z + (my_z + dz) % n_z

    steps = [1, -1, 2, -2]
    column = list(range(1, n_z))
    for dz in column:
        pl.semaphore_signal(barrier, inc=1, device_id={"spec": at(0, dz)}, device_id_type=MESH)
    for dy in (1, -1):
        pl.semaphore_signal(barrier, inc=1, device_id={"spec": at(dy, 0)}, device_id_type=MESH)
    for step in steps:
        pl.semaphore_signal(barrier, inc=1, device_id={"tile": (tile + step + n_tile) % n_tile}, device_id_type=MESH)

    named = [jnp.int32(0)] * 5
    for j in range(active.shape[0]):
        home = (dest[j] - tile + n_tile + n_tile // 2) % n_tile - n_tile // 2
        valid = active[j] < out.shape[1] // BLK
        for i, step in enumerate([0] + steps):
            named[i] = named[i] + jnp.where(valid & (home == step), 1, 0)
    for i in range(5):
        counts[i] = jnp.full(counts.shape[1:], named[i], jnp.int32)

    for copy in loads:
        copy.wait()
    for c in range(halves):
        half_rest[c, PAD : PAD + rows] = 0.5 * (1.0 - rate[c, PAD : PAD + rows])

    sides = [(PAD + rows - 4, 4, 4, up), (PAD, PAD + rows, 2, down)]
    for index, (origin, _, thick, _) in enumerate(sides):
        for c in range(halves):
            for s in range(species):
                field_out[index, c, s * thick : (s + 1) * thick] = field[c, s * deep + origin : s * deep + origin + thick]

    def advect(d):
        first = PAD + d * share_rows
        finished = []
        for c in range(halves):
            def value(i):
                return field[c, pl.ds(first + i, species, stride=deep), :]

            def rates(i):
                return rate[c, pl.ds(first + i, 1), :], half_rest[c, pl.ds(first + i, 1), :]

            def flux(i, mid, left, right):
                speed, rest = rates(i)
                return speed * (mid + rest * minmod(left, right))

            before, mid = value(-4), value(-3)
            left = mid - before
            flow, once = None, {}
            done = []
            previous, left2, flow2 = None, None, None
            for i in range(-3, share_rows + 1):
                after = value(i + 1)
                right = after - mid
                now = flux(i, mid, left, right)
                if flow is not None:
                    fresh = mid - now + flow
                    once[i] = fresh
                    if i - 1 in once:
                        right2 = fresh - once[i - 1]
                        if left2 is not None:
                            now2 = flux(i - 1, once[i - 1], left2, right2)
                            if flow2 is not None:
                                done.append(once[i - 1] - now2 + flow2)
                            flow2 = now2
                        left2 = right2
                flow, mid, left = now, after, right
            finished.append(done)
        for r in range(share_rows):
            both = jnp.concatenate([finished[c][r] for c in range(halves)], axis=1)
            spot = (r % per_group) * width
            send[d, r // per_group, :, spot : spot + width] = both.astype(BF16)

    def inside(d):
        return (d != 0) & (d != n_spec - 1)

    def first(dz, carry):
        @pl.when(inside(at(0, dz)))
        def _():
            advect(at(0, dz))
        return carry

    lax.fori_loop(1, n_z, first, 0)

    pl.semaphore_wait(barrier, len(column) + 2 + len(steps))

    def message(d, g):
        return pltpu.make_async_remote_copy(
            send.at[d, g], recv.at[g, me], send_sem, recv_sem.at[g], device_id={"spec": d}, device_id_type=MESH)

    for dz in column:
        @pl.when(inside(at(0, dz)))
        def _(d=at(0, dz)):
            def every(g, carry):
                message(d, g).start()
                return carry

            lax.fori_loop(0, n_group, every, 0)

    halo = []
    for index, (_, _, thick, device) in enumerate(sides):
        for c in range(halves):
            halo.append(pltpu.make_async_remote_copy(
                field_out.at[index, c, pl.ds(0, species * thick)], field_in.at[index, c, pl.ds(0, species * thick)],
                halo_send.at[2 * c + index], halo_recv.at[2 * c + index], device_id={"tile": device}, device_id_type=MESH))
            halo.append(pltpu.make_async_remote_copy(
                rate.at[c, pl.ds(PAD + (rows - PAD if index == 0 else 0), PAD), :], rate_in.at[index, c],
                halo_send.at[4 + 2 * c + index], halo_recv.at[4 + 2 * c + index], device_id={"tile": device}, device_id_type=MESH))
    for copy in halo:
        copy.start()
    tallies = []
    for i, step in enumerate(steps):
        tallies.append(pltpu.make_async_remote_copy(
            counts.at[i + 1], counts_in.at[i], count_send.at[i], count_recv.at[i],
            device_id={"tile": (tile + step + n_tile) % n_tile}, device_id_type=MESH))
    for copy in tallies:
        copy.start()

    farthest = n_y // 2

    def stage(reach, carry):
        for way, dy in enumerate((1, -1)):
            pl.semaphore_signal(known.at[reach - 1, way], inc=1, device_id={"spec": at(dy, 0)}, device_id_type=MESH)

        def piece(i):
            return at(jnp.where(i < n_z, reach, -reach), i + 1)

        def sweep(i, carry):
            alone = (reach == farthest) & (i == n_z)
            d = jnp.where(alone, me, piece(i))

            @pl.when(inside(d) & ((reach < farthest) | (i <= n_z)))
            def _():
                advect(d)
            return carry

        lax.fori_loop(0, 2 * n_z, sweep, 0)
        for way in range(2):
            pl.semaphore_wait(known.at[reach - 1, way], 1)

        def post(i, carry):
            @pl.when(inside(piece(i)) & ((reach < farthest) | (i < n_z)))
            def _():
                message(piece(i), 0).start()
            return carry

        lax.fori_loop(0, 2 * n_z, post, 0)
        return carry

    lax.fori_loop(1, farthest + 1, stage, 0)

    for copy in halo:
        copy.wait()
    for c in range(halves):
        for index, (_, target, thick, _) in enumerate(sides):
            base = index * (PAD + rows)
            rate[c, base : base + PAD] = rate_in[index, c]
            for s in range(species):
                field[c, s * deep + target : s * deep + target + thick] = field_in[index, c, s * thick : (s + 1) * thick]
            half_rest[c, base : base + PAD] = 0.5 * (1.0 - rate[c, base : base + PAD])

    def edge(e, carry):
        d = e * (n_spec - 1)
        advect(d)

        @pl.when(d != me)
        def _():
            message(d, 0).start()
        return carry

    lax.fori_loop(0, 2, edge, 0)

    def later(i, carry):
        g, k = i // (n_spec - 1), i % (n_spec - 1) + 1
        d = partner(k)

        @pl.when((k % n_y != 0) | (d == 0) | (d == n_spec - 1))
        def _():
            message(d, g).start()
        return carry

    lax.fori_loop(n_spec - 1, n_group * (n_spec - 1), later, 0)

    own = pltpu.make_async_copy(send.at[me], recv.at[:, me], own_sem)
    own.start()

    for copy in weights:
        copy.wait()
    w1_t[...] = (w1[...] * BF16(0.5)).T
    w2_t[...] = (w2[...] * BF16(0.5)).T
    own.wait()

    span = recv.shape[3]
    total = n_spec * species

    def integrate(g, carry):
        pltpu.make_async_remote_copy(
            recv.at[g, pl.ds(0, n_spec - 1)], recv.at[g, pl.ds(0, n_spec - 1)], send_sem, recv_sem.at[g],
            device_id={"spec": me}, device_id_type=MESH).wait_recv()
        x = recv[g].reshape(total, span)
        one = fused_silu(jnp.dot(w1_t[...], x, preferred_element_type=F32))
        two = fused_silu(jnp.dot(w2_t[...], one, preferred_element_type=F32))
        change = jnp.dot(w3_t[...], two, preferred_element_type=F32)
        fresh = (x.astype(F32) + change).astype(BF16)
        for b in range(span // BLK):
            block = g * (span // BLK) + b
            listed = jnp.int32(0)
            for j in range(active.shape[0]):
                listed = listed + jnp.where(active[j] == block, 1, 0)
            cols = slice(b * BLK, (b + 1) * BLK)
            chosen = jnp.where(jnp.full((total, BLK), listed, jnp.int32) > 0, fresh[:, cols].astype(F32), x[:, cols].astype(F32))
            out[:, pl.ds(pl.multiple_of(block * BLK, BLK), BLK)] = chosen.astype(BF16)
        return carry

    lax.fori_loop(0, n_group, integrate, 0)

    for copy in tallies:
        copy.wait()
    tally = counts[0] + counts_in[0] + counts_in[1] + counts_in[2] + counts_in[3]
    share[...] = tally[0:1, 0:1].astype(F32) / RECV

    pltpu.make_async_remote_copy(
        recv.at[:, pl.ds(0, n_spec - 1)], recv.at[:, pl.ds(0, n_spec - 1)], send_sem, own_sem,
        device_id={"spec": me}, device_id_type=MESH).wait_send()


def solution(mesh):
    n_tile, n_spec = mesh.shape["tile"], mesh.shape["spec"]

    def shards(conc, courant, w1, w2, w3, active, dest):
        species, rows, width = conc.shape
        hidden = w2.shape[0]
        halves = width // BLK
        total = n_spec * species
        cells = rows // n_spec * width
        span = cells // GROUPS
        deep = rows + 2 * PAD
        anywhere = pl.BlockSpec(memory_space=pl.ANY)
        scalars = pl.BlockSpec(memory_space=pltpu.SMEM)
        vector = pl.BlockSpec(memory_space=pltpu.VMEM)
        out, share = pl.pallas_call(
            functools.partial(kernel, n_tile, n_spec, 3, GROUPS),
            out_shape=(pltpu.VMEM((total, cells), BF16), jax.ShapeDtypeStruct((1, 1), F32)),
            in_specs=[anywhere] * 5 + [scalars] * 2,
            out_specs=(vector, vector),
            scratch_shapes=[
                pltpu.VMEM((halves, species * deep, BLK), F32),
                pltpu.VMEM((halves, deep, BLK), F32),
                pltpu.VMEM((halves, deep, BLK), F32),
                pltpu.VMEM((2, halves, species * 4, BLK), F32),
                pltpu.VMEM((2, halves, species * 4, BLK), F32),
                pltpu.VMEM((2, halves, PAD, BLK), F32),
                pltpu.VMEM((n_spec, GROUPS, species, span), BF16),
                pltpu.VMEM((GROUPS, n_spec, species, span), BF16),
                pltpu.VMEM((total, hidden), BF16),
                pltpu.VMEM((hidden, hidden), BF16),
                pltpu.VMEM((hidden, total), BF16),
                pltpu.VMEM((hidden, hidden), BF16),
                pltpu.VMEM((total, hidden), BF16),
                pltpu.VMEM((5, 8, BLK), jnp.int32),
                pltpu.VMEM((4, 8, BLK), jnp.int32),
                pltpu.SemaphoreType.DMA((2 * halves,)),
                pltpu.SemaphoreType.DMA((3,)),
                pltpu.SemaphoreType.DMA((4 * halves,)),
                pltpu.SemaphoreType.DMA((4 * halves,)),
                pltpu.SemaphoreType.DMA((4,)),
                pltpu.SemaphoreType.DMA((4,)),
                pltpu.SemaphoreType.DMA,
                pltpu.SemaphoreType.DMA((GROUPS,)),
                pltpu.SemaphoreType.DMA,
                pltpu.SemaphoreType.REGULAR((max(n_spec // 6, 1), 2)),
            ],
            compiler_params=pltpu.CompilerParams(
                collective_id=0, has_side_effects=True, vmem_limit_bytes=60 * 1024 * 1024
            ),
            name="sweep_exchange_chemistry",
        )(conc, courant, w1, w2, w3.T, active.reshape(-1), dest.reshape(-1))
        return out, share

    in_specs = (
        P("spec", "tile", None),
        P("tile", None),
        P(),
        P(),
        P(),
        P("tile", "spec", None),
        P("tile", "spec", None),
    )
    out_specs = (P(None, ("tile", "spec")), P("tile", "spec"))
    return jax.shard_map(shards, mesh=mesh, in_specs=in_specs, out_specs=out_specs, check_vma=False)
```

```python
import functools

import jax
import jax.numpy as jnp
from jax import lax
from jax.experimental import pallas as pl
from jax.experimental.pallas import tpu as pltpu
from jax.sharding import PartitionSpec as P

BLK = 128
RECV = 8
NBR = 2
GROUPS = 8
PAD = 8
MESH = pl.DeviceIdType.MESH
F32 = jnp.float32
BF16 = jnp.bfloat16


def minmod(left, right):
    return jnp.maximum(jnp.minimum(left, right), 0.0) + jnp.minimum(jnp.maximum(left, right), 0.0)


def fused_silu(half):
    return (half + half * jnp.tanh(half)).astype(BF16)


def kernel(
    n_tile, n_spec, n_z, n_group,
    conc, courant, w1_hbm, w2_hbm, w3_hbm, active_hbm, dest_hbm,
    out, share,
    field, rate, half_rest, field_out, field_in, rate_in, send, recv, w1, w2, w1_t, w2_t, w3_t, counts, counts_in, active, dest,
    load_sem, weight_sem, halo_send, halo_recv, count_send, count_recv, send_sem, recv_sem, own_sem, known,
):
    tile = lax.axis_index("tile")
    me = lax.axis_index("spec")
    my_y, my_z = me // n_z, me % n_z
    n_y = n_spec // n_z
    rows = conc.shape[1]
    deep = rows + 2 * PAD
    share_rows = rows // n_spec
    width = conc.shape[2]
    halves = width // BLK
    per_group = share_rows // n_group
    up, down = (tile + 1) % n_tile, (tile + n_tile - 1) % n_tile

    def partner(k):
        return ((my_y + k) % n_y) * n_z + (my_z + k) % n_z

    barrier = pltpu.get_barrier_semaphore()

    def at(dy, dz):
        return ((my_y + dy + n_y) % n_y) * n_z + (my_z + dz) % n_z

    steps = [1, -1, 2, -2]
    column = list(range(1, n_z))
    for dz in column:
        pl.semaphore_signal(barrier, inc=1, device_id={"spec": at(0, dz)}, device_id_type=MESH)
    for dy in (1, -1):
        pl.semaphore_signal(barrier, inc=1, device_id={"spec": at(dy, 0)}, device_id_type=MESH)
    for step in steps:
        pl.semaphore_signal(barrier, inc=1, device_id={"tile": (tile + step + n_tile) % n_tile}, device_id_type=MESH)

    species = conc.shape[0]

    def load(s, carry):
        for c in range(halves):
            pltpu.make_async_copy(
                conc.at[s, :, pl.ds(c * BLK, BLK)], field.at[c, pl.ds(pl.multiple_of(s * deep + PAD, PAD), rows), :], load_sem.at[c]
            ).start()
        return carry

    lax.fori_loop(0, species, load, 0)
    loads = []
    for c in range(halves):
        loads.append(pltpu.make_async_copy(
            courant.at[:, pl.ds(c * BLK, BLK)], rate.at[c, pl.ds(PAD, rows), :], load_sem.at[halves + c]))
        loads[-1].start()
        whole = field.at[c, pl.ds(0, species * rows), :]
        loads.append(pltpu.make_async_copy(whole, whole, load_sem.at[c]))
    weights = [
        pltpu.make_async_copy(w1_hbm, w1, weight_sem.at[0]),
        pltpu.make_async_copy(w2_hbm, w2, weight_sem.at[1]),
        pltpu.make_async_copy(w3_hbm, w3_t, weight_sem.at[2]),
    ]
    lists = [
        pltpu.make_async_copy(active_hbm, active, weight_sem.at[3]),
        pltpu.make_async_copy(dest_hbm, dest, weight_sem.at[4]),
    ]
    for copy in lists + weights:
        copy.start()

    for copy in loads:
        copy.wait()
    for c in range(halves):
        half_rest[c, PAD : PAD + rows] = 0.5 * (1.0 - rate[c, PAD : PAD + rows])

    sides = [(PAD + rows - 4, 4, 4, up), (PAD, PAD + rows, 2, down)]
    for index, (origin, _, thick, _) in enumerate(sides):
        for c in range(halves):
            for s in range(species):
                field_out[index, c, s * thick : (s + 1) * thick] = field[c, s * deep + origin : s * deep + origin + thick]

    def advect(d):
        first = PAD + d * share_rows
        finished = []
        for c in range(halves):
            def value(i):
                return field[c, pl.ds(first + i, species, stride=deep), :]

            def rates(i):
                return rate[c, pl.ds(first + i, 1), :], half_rest[c, pl.ds(first + i, 1), :]

            def flux(i, mid, left, right):
                speed, rest = rates(i)
                return speed * (mid + rest * minmod(left, right))

            before, mid = value(-4), value(-3)
            left = mid - before
            flow, once = None, {}
            done = []
            previous, left2, flow2 = None, None, None
            for i in range(-3, share_rows + 1):
                after = value(i + 1)
                right = after - mid
                now = flux(i, mid, left, right)
                if flow is not None:
                    fresh = mid - now + flow
                    once[i] = fresh
                    if i - 1 in once:
                        right2 = fresh - once[i - 1]
                        if left2 is not None:
                            now2 = flux(i - 1, once[i - 1], left2, right2)
                            if flow2 is not None:
                                done.append(once[i - 1] - now2 + flow2)
                            flow2 = now2
                        left2 = right2
                flow, mid, left = now, after, right
            finished.append(done)
        for r in range(share_rows):
            both = jnp.concatenate([finished[c][r] for c in range(halves)], axis=1)
            spot = (r % per_group) * width
            send[d, r // per_group, :, spot : spot + width] = both.astype(BF16)

    def inside(d):
        return (d != 0) & (d != n_spec - 1)

    def first(dz, carry):
        @pl.when(inside(at(0, dz)))
        def _():
            advect(at(0, dz))
        return carry

    lax.fori_loop(1, n_z, first, 0)

    pl.semaphore_wait(barrier, len(column) + 2 + len(steps))

    def message(d, g):
        return pltpu.make_async_remote_copy(
            send.at[d, g], recv.at[g, me], send_sem, recv_sem.at[g], device_id={"spec": d}, device_id_type=MESH)

    for dz in column:
        @pl.when(inside(at(0, dz)))
        def _(d=at(0, dz)):
            def every(g, carry):
                message(d, g).start()
                return carry

            lax.fori_loop(0, n_group, every, 0)

    halo = []
    for index, (_, _, thick, device) in enumerate(sides):
        for c in range(halves):
            halo.append(pltpu.make_async_remote_copy(
                field_out.at[index, c, pl.ds(0, species * thick)], field_in.at[index, c, pl.ds(0, species * thick)],
                halo_send.at[2 * c + index], halo_recv.at[2 * c + index], device_id={"tile": device}, device_id_type=MESH))
            halo.append(pltpu.make_async_remote_copy(
                rate.at[c, pl.ds(PAD + (rows - PAD if index == 0 else 0), PAD), :], rate_in.at[index, c],
                halo_send.at[4 + 2 * c + index], halo_recv.at[4 + 2 * c + index], device_id={"tile": device}, device_id_type=MESH))
    for copy in halo:
        copy.start()
    for copy in lists:
        copy.wait()
    named = [jnp.int32(0)] * 5
    for j in range(active.shape[0]):
        home = (dest[j] - tile + n_tile + n_tile // 2) % n_tile - n_tile // 2
        valid = active[j] < out.shape[1] // BLK
        for i, step in enumerate([0] + steps):
            named[i] = named[i] + jnp.where(valid & (home == step), 1, 0)
    for i in range(5):
        counts[i] = jnp.full(counts.shape[1:], named[i], jnp.int32)

    tallies = []
    for i, step in enumerate(steps):
        tallies.append(pltpu.make_async_remote_copy(
            counts.at[i + 1], counts_in.at[i], count_send.at[i], count_recv.at[i],
            device_id={"tile": (tile + step + n_tile) % n_tile}, device_id_type=MESH))
    for copy in tallies:
        copy.start()

    farthest = n_y // 2

    def stage(reach, carry):
        for way, dy in enumerate((1, -1)):
            pl.semaphore_signal(known.at[reach - 1, way], inc=1, device_id={"spec": at(dy, 0)}, device_id_type=MESH)

        def piece(i):
            return at(jnp.where(i < n_z, reach, -reach), i + 1)

        def sweep(i, carry):
            alone = (reach == farthest) & (i == n_z)
            d = jnp.where(alone, me, piece(i))

            @pl.when(inside(d) & ((reach < farthest) | (i <= n_z)))
            def _():
                advect(d)
            return carry

        lax.fori_loop(0, 2 * n_z, sweep, 0)
        for way in range(2):
            pl.semaphore_wait(known.at[reach - 1, way], 1)

        def post(i, carry):
            @pl.when(inside(piece(i)) & ((reach < farthest) | (i < n_z)))
            def _():
                message(piece(i), 0).start()
            return carry

        lax.fori_loop(0, 2 * n_z, post, 0)
        return carry

    lax.fori_loop(1, farthest + 1, stage, 0)

    for copy in halo:
        copy.wait()
    for c in range(halves):
        for index, (_, target, thick, _) in enumerate(sides):
            base = index * (PAD + rows)
            rate[c, base : base + PAD] = rate_in[index, c]
            for s in range(species):
                field[c, s * deep + target : s * deep + target + thick] = field_in[index, c, s * thick : (s + 1) * thick]
            half_rest[c, base : base + PAD] = 0.5 * (1.0 - rate[c, base : base + PAD])

    def edge(e, carry):
        d = e * (n_spec - 1)
        advect(d)

        @pl.when(d != me)
        def _():
            message(d, 0).start()
        return carry

    lax.fori_loop(0, 2, edge, 0)

    def later(i, carry):
        g, k = i // (n_spec - 1), i % (n_spec - 1) + 1
        d = partner(k)

        @pl.when((k % n_y != 0) | (d == 0) | (d == n_spec - 1))
        def _():
            message(d, g).start()
        return carry

    lax.fori_loop(n_spec - 1, n_group * (n_spec - 1), later, 0)

    own = pltpu.make_async_copy(send.at[me], recv.at[:, me], own_sem)
    own.start()

    for copy in weights:
        copy.wait()
    w1_t[...] = (w1[...] * BF16(0.5)).T
    w2_t[...] = (w2[...] * BF16(0.5)).T
    own.wait()

    span = recv.shape[3]
    total = n_spec * species

    def integrate(g, carry):
        pltpu.make_async_remote_copy(
            recv.at[g, pl.ds(0, n_spec - 1)], recv.at[g, pl.ds(0, n_spec - 1)], send_sem, recv_sem.at[g],
            device_id={"spec": me}, device_id_type=MESH).wait_recv()
        x = recv[g].reshape(total, span)
        one = fused_silu(jnp.dot(w1_t[...], x, preferred_element_type=F32))
        two = fused_silu(jnp.dot(w2_t[...], one, preferred_element_type=F32))
        change = jnp.dot(w3_t[...], two, preferred_element_type=F32)
        fresh = (x.astype(F32) + change).astype(BF16)
        for b in range(span // BLK):
            block = g * (span // BLK) + b
            listed = jnp.int32(0)
            for j in range(active.shape[0]):
                listed = listed + jnp.where(active[j] == block, 1, 0)
            cols = slice(b * BLK, (b + 1) * BLK)
            chosen = jnp.where(jnp.full((total, BLK), listed, jnp.int32) > 0, fresh[:, cols].astype(F32), x[:, cols].astype(F32))
            out[:, pl.ds(pl.multiple_of(block * BLK, BLK), BLK)] = chosen.astype(BF16)
        return carry

    lax.fori_loop(0, n_group, integrate, 0)

    for copy in tallies:
        copy.wait()
    tally = counts[0] + counts_in[0] + counts_in[1] + counts_in[2] + counts_in[3]
    share[...] = tally[0:1, 0:1].astype(F32) / RECV

    pltpu.make_async_remote_copy(
        recv.at[:, pl.ds(0, n_spec - 1)], recv.at[:, pl.ds(0, n_spec - 1)], send_sem, own_sem,
        device_id={"spec": me}, device_id_type=MESH).wait_send()


def solution(mesh):
    n_tile, n_spec = mesh.shape["tile"], mesh.shape["spec"]

    def shards(conc, courant, w1, w2, w3, active, dest):
        species, rows, width = conc.shape
        hidden = w2.shape[0]
        halves = width // BLK
        total = n_spec * species
        cells = rows // n_spec * width
        span = cells // GROUPS
        deep = rows + 2 * PAD
        anywhere = pl.BlockSpec(memory_space=pl.ANY)
        vector = pl.BlockSpec(memory_space=pltpu.VMEM)
        out, share = pl.pallas_call(
            functools.partial(kernel, n_tile, n_spec, 3, GROUPS),
            out_shape=(pltpu.VMEM((total, cells), BF16), pltpu.VMEM((1, 1), F32)),
            in_specs=[anywhere] * 7,
            out_specs=(vector, vector),
            scratch_shapes=[
                pltpu.VMEM((halves, species * deep, BLK), F32),
                pltpu.VMEM((halves, deep, BLK), F32),
                pltpu.VMEM((halves, deep, BLK), F32),
                pltpu.VMEM((2, halves, species * 4, BLK), F32),
                pltpu.VMEM((2, halves, species * 4, BLK), F32),
                pltpu.VMEM((2, halves, PAD, BLK), F32),
                pltpu.VMEM((n_spec, GROUPS, species, span), BF16),
                pltpu.VMEM((GROUPS, n_spec, species, span), BF16),
                pltpu.VMEM((total, hidden), BF16),
                pltpu.VMEM((hidden, hidden), BF16),
                pltpu.VMEM((hidden, total), BF16),
                pltpu.VMEM((hidden, hidden), BF16),
                pltpu.VMEM((total, hidden), BF16),
                pltpu.VMEM((5, 8, BLK), jnp.int32),
                pltpu.VMEM((4, 8, BLK), jnp.int32),
                pltpu.SMEM((active.size,), jnp.int32),
                pltpu.SMEM((dest.size,), jnp.int32),
                pltpu.SemaphoreType.DMA((2 * halves,)),
                pltpu.SemaphoreType.DMA((5,)),
                pltpu.SemaphoreType.DMA((4 * halves,)),
                pltpu.SemaphoreType.DMA((4 * halves,)),
                pltpu.SemaphoreType.DMA((4,)),
                pltpu.SemaphoreType.DMA((4,)),
                pltpu.SemaphoreType.DMA,
                pltpu.SemaphoreType.DMA((GROUPS,)),
                pltpu.SemaphoreType.DMA,
                pltpu.SemaphoreType.REGULAR((max(n_spec // 6, 1), 2)),
            ],
            compiler_params=pltpu.CompilerParams(
                collective_id=0, has_side_effects=True, vmem_limit_bytes=60 * 1024 * 1024
            ),
            name="sweep_exchange_chemistry",
        )(conc, courant, w1, w2, w3.T, active.reshape(-1), dest.reshape(-1))
        return out, share

    in_specs = (
        P("spec", "tile", None),
        P("tile", None),
        P(),
        P(),
        P(),
        P("tile", "spec", None),
        P("tile", "spec", None),
    )
    out_specs = (P(None, ("tile", "spec")), P("tile", "spec"))
    return jax.shard_map(shards, mesh=mesh, in_specs=in_specs, out_specs=out_specs, check_vma=False)
```

```python
import functools

import jax
import jax.numpy as jnp
from jax import lax
from jax.experimental import pallas as pl
from jax.experimental.pallas import tpu as pltpu
from jax.sharding import PartitionSpec as P

BLK = 128
RECV = 8
NBR = 2
GROUPS = 8
PAD = 8
MESH = pl.DeviceIdType.MESH
F32 = jnp.float32
BF16 = jnp.bfloat16


def minmod(left, right):
    return jnp.maximum(jnp.minimum(left, right), 0.0) + jnp.minimum(jnp.maximum(left, right), 0.0)


def fused_silu(half):
    return (half + half * jnp.tanh(half)).astype(BF16)


def kernel(
    n_tile, n_spec, n_z, n_group,
    conc, courant, w1_hbm, w2_hbm, w3_hbm, active_hbm, dest_hbm,
    out, share,
    field, rate, half_rest, field_out, field_in, rate_in, send, recv, w1, w2, w1_t, w2_t, w3_t, counts, counts_in, active, dest,
    load_sem, weight_sem, halo_send, halo_recv, count_send, count_recv, send_sem, recv_sem, own_sem, known,
):
    tile = lax.axis_index("tile")
    me = lax.axis_index("spec")
    my_y, my_z = me // n_z, me % n_z
    n_y = n_spec // n_z
    rows = conc.shape[1]
    deep = rows + 2 * PAD
    share_rows = rows // n_spec
    width = conc.shape[2]
    halves = width // BLK
    per_group = share_rows // n_group
    up, down = (tile + 1) % n_tile, (tile + n_tile - 1) % n_tile

    def partner(k):
        return ((my_y + k) % n_y) * n_z + (my_z + k) % n_z

    barrier = pltpu.get_barrier_semaphore()

    def at(dy, dz):
        return ((my_y + dy + n_y) % n_y) * n_z + (my_z + dz) % n_z

    steps = [1, -1, 2, -2]
    column = list(range(1, n_z))
    for dz in column:
        pl.semaphore_signal(barrier, inc=1, device_id={"spec": at(0, dz)}, device_id_type=MESH)
    for dy in (1, -1):
        pl.semaphore_signal(barrier, inc=1, device_id={"spec": at(dy, 0)}, device_id_type=MESH)
    for step in steps:
        pl.semaphore_signal(barrier, inc=1, device_id={"tile": (tile + step + n_tile) % n_tile}, device_id_type=MESH)

    species = conc.shape[0]

    def load(s, carry):
        for c in range(halves):
            pltpu.make_async_copy(
                conc.at[s, :, pl.ds(c * BLK, BLK)], field.at[c, pl.ds(pl.multiple_of(s * deep + PAD, PAD), rows), :], load_sem.at[c]
            ).start()
        return carry

    lax.fori_loop(0, species, load, 0)
    loads = []
    for c in range(halves):
        loads.append(pltpu.make_async_copy(
            courant.at[:, pl.ds(c * BLK, BLK)], rate.at[c, pl.ds(PAD, rows), :], load_sem.at[halves + c]))
        loads[-1].start()
        whole = field.at[c, pl.ds(0, species * rows), :]
        loads.append(pltpu.make_async_copy(whole, whole, load_sem.at[c]))
    weights = [
        pltpu.make_async_copy(w1_hbm, w1, weight_sem.at[0]),
        pltpu.make_async_copy(w2_hbm, w2, weight_sem.at[1]),
        pltpu.make_async_copy(w3_hbm, w3_t, weight_sem.at[2]),
    ]
    lists = [
        pltpu.make_async_copy(active_hbm, active, weight_sem.at[3]),
        pltpu.make_async_copy(dest_hbm, dest, weight_sem.at[4]),
    ]

    for copy in loads:
        copy.wait()
    for c in range(halves):
        half_rest[c, PAD : PAD + rows] = 0.5 * (1.0 - rate[c, PAD : PAD + rows])

    sides = [(PAD + rows - 4, 4, 4, up), (PAD, PAD + rows, 2, down)]
    def advect(d):
        first = PAD + d * share_rows
        finished = []
        for c in range(halves):
            def value(i):
                return field[c, pl.ds(first + i, species, stride=deep), :]

            def rates(i):
                return rate[c, pl.ds(first + i, 1), :], half_rest[c, pl.ds(first + i, 1), :]

            def flux(i, mid, left, right):
                speed, rest = rates(i)
                return speed * (mid + rest * minmod(left, right))

            before, mid = value(-4), value(-3)
            left = mid - before
            flow, once = None, {}
            done = []
            previous, left2, flow2 = None, None, None
            for i in range(-3, share_rows + 1):
                after = value(i + 1)
                right = after - mid
                now = flux(i, mid, left, right)
                if flow is not None:
                    fresh = mid - now + flow
                    once[i] = fresh
                    if i - 1 in once:
                        right2 = fresh - once[i - 1]
                        if left2 is not None:
                            now2 = flux(i - 1, once[i - 1], left2, right2)
                            if flow2 is not None:
                                done.append(once[i - 1] - now2 + flow2)
                            flow2 = now2
                        left2 = right2
                flow, mid, left = now, after, right
            finished.append(done)
        for r in range(share_rows):
            both = jnp.concatenate([finished[c][r] for c in range(halves)], axis=1)
            spot = (r % per_group) * width
            send[d, r // per_group, :, spot : spot + width] = both.astype(BF16)

    def inside(d):
        return (d != 0) & (d != n_spec - 1)

    def first(dz, carry):
        @pl.when(inside(at(0, dz)))
        def _():
            advect(at(0, dz))
        return carry

    lax.fori_loop(1, n_z, first, 0)

    pl.semaphore_wait(barrier, len(column) + 2 + len(steps))

    def message(d, g):
        return pltpu.make_async_remote_copy(
            send.at[d, g], recv.at[g, me], send_sem, recv_sem.at[g], device_id={"spec": d}, device_id_type=MESH)

    for dz in column:
        @pl.when(inside(at(0, dz)))
        def _(d=at(0, dz)):
            def every(g, carry):
                message(d, g).start()
                return carry

            lax.fori_loop(0, n_group, every, 0)

    for copy in lists + weights:
        copy.start()
    for index, (origin, _, thick, _) in enumerate(sides):
        for c in range(halves):
            for s in range(species):
                field_out[index, c, s * thick : (s + 1) * thick] = field[c, s * deep + origin : s * deep + origin + thick]

    halo = []
    for index, (_, _, thick, device) in enumerate(sides):
        for c in range(halves):
            halo.append(pltpu.make_async_remote_copy(
                field_out.at[index, c, pl.ds(0, species * thick)], field_in.at[index, c, pl.ds(0, species * thick)],
                halo_send.at[2 * c + index], halo_recv.at[2 * c + index], device_id={"tile": device}, device_id_type=MESH))
            halo.append(pltpu.make_async_remote_copy(
                rate.at[c, pl.ds(PAD + (rows - PAD if index == 0 else 0), PAD), :], rate_in.at[index, c],
                halo_send.at[4 + 2 * c + index], halo_recv.at[4 + 2 * c + index], device_id={"tile": device}, device_id_type=MESH))
    for copy in halo:
        copy.start()
    for copy in lists:
        copy.wait()
    named = [jnp.int32(0)] * 5
    for j in range(active.shape[0]):
        home = (dest[j] - tile + n_tile + n_tile // 2) % n_tile - n_tile // 2
        valid = active[j] < out.shape[1] // BLK
        for i, step in enumerate([0] + steps):
            named[i] = named[i] + jnp.where(valid & (home == step), 1, 0)
    for i in range(5):
        counts[i] = jnp.full(counts.shape[1:], named[i], jnp.int32)

    tallies = []
    for i, step in enumerate(steps):
        tallies.append(pltpu.make_async_remote_copy(
            counts.at[i + 1], counts_in.at[i], count_send.at[i], count_recv.at[i],
            device_id={"tile": (tile + step + n_tile) % n_tile}, device_id_type=MESH))
    for copy in tallies:
        copy.start()

    farthest = n_y // 2

    def stage(reach, carry):
        for way, dy in enumerate((1, -1)):
            pl.semaphore_signal(known.at[reach - 1, way], inc=1, device_id={"spec": at(dy, 0)}, device_id_type=MESH)

        def piece(i):
            return at(jnp.where(i < n_z, reach, -reach), i + 1)

        def sweep(i, carry):
            alone = (reach == farthest) & (i == n_z)
            d = jnp.where(alone, me, piece(i))

            @pl.when(inside(d) & ((reach < farthest) | (i <= n_z)))
            def _():
                advect(d)
            return carry

        lax.fori_loop(0, 2 * n_z, sweep, 0)
        for way in range(2):
            pl.semaphore_wait(known.at[reach - 1, way], 1)

        def post(i, carry):
            @pl.when(inside(piece(i)) & ((reach < farthest) | (i < n_z)))
            def _():
                message(piece(i), 0).start()
            return carry

        lax.fori_loop(0, 2 * n_z, post, 0)
        return carry

    lax.fori_loop(1, farthest + 1, stage, 0)

    for copy in halo:
        copy.wait()
    for c in range(halves):
        for index, (_, target, thick, _) in enumerate(sides):
            base = index * (PAD + rows)
            rate[c, base : base + PAD] = rate_in[index, c]
            for s in range(species):
                field[c, s * deep + target : s * deep + target + thick] = field_in[index, c, s * thick : (s + 1) * thick]
            half_rest[c, base : base + PAD] = 0.5 * (1.0 - rate[c, base : base + PAD])

    def edge(e, carry):
        d = e * (n_spec - 1)
        advect(d)

        @pl.when(d != me)
        def _():
            message(d, 0).start()
        return carry

    lax.fori_loop(0, 2, edge, 0)

    def later(i, carry):
        g, k = i // (n_spec - 1), i % (n_spec - 1) + 1
        d = partner(k)

        @pl.when((k % n_y != 0) | (d == 0) | (d == n_spec - 1))
        def _():
            message(d, g).start()
        return carry

    lax.fori_loop(n_spec - 1, n_group * (n_spec - 1), later, 0)

    own = pltpu.make_async_copy(send.at[me], recv.at[:, me], own_sem)
    own.start()

    for copy in weights:
        copy.wait()
    w1_t[...] = (w1[...] * BF16(0.5)).T
    w2_t[...] = (w2[...] * BF16(0.5)).T
    own.wait()

    span = recv.shape[3]
    total = n_spec * species

    def integrate(g, carry):
        pltpu.make_async_remote_copy(
            recv.at[g, pl.ds(0, n_spec - 1)], recv.at[g, pl.ds(0, n_spec - 1)], send_sem, recv_sem.at[g],
            device_id={"spec": me}, device_id_type=MESH).wait_recv()
        x = recv[g].reshape(total, span)
        one = fused_silu(jnp.dot(w1_t[...], x, preferred_element_type=F32))
        two = fused_silu(jnp.dot(w2_t[...], one, preferred_element_type=F32))
        change = jnp.dot(w3_t[...], two, preferred_element_type=F32)
        fresh = (x.astype(F32) + change).astype(BF16)
        for b in range(span // BLK):
            block = g * (span // BLK) + b
            listed = jnp.int32(0)
            for j in range(active.shape[0]):
                listed = listed + jnp.where(active[j] == block, 1, 0)
            cols = slice(b * BLK, (b + 1) * BLK)
            chosen = jnp.where(jnp.full((total, BLK), listed, jnp.int32) > 0, fresh[:, cols].astype(F32), x[:, cols].astype(F32))
            out[:, pl.ds(pl.multiple_of(block * BLK, BLK), BLK)] = chosen.astype(BF16)
        return carry

    lax.fori_loop(0, n_group, integrate, 0)

    for copy in tallies:
        copy.wait()
    tally = counts[0] + counts_in[0] + counts_in[1] + counts_in[2] + counts_in[3]
    share[...] = tally[0:1, 0:1].astype(F32) / RECV

    pltpu.make_async_remote_copy(
        recv.at[:, pl.ds(0, n_spec - 1)], recv.at[:, pl.ds(0, n_spec - 1)], send_sem, own_sem,
        device_id={"spec": me}, device_id_type=MESH).wait_send()


def solution(mesh):
    n_tile, n_spec = mesh.shape["tile"], mesh.shape["spec"]

    def shards(conc, courant, w1, w2, w3, active, dest):
        species, rows, width = conc.shape
        hidden = w2.shape[0]
        halves = width // BLK
        total = n_spec * species
        cells = rows // n_spec * width
        span = cells // GROUPS
        deep = rows + 2 * PAD
        anywhere = pl.BlockSpec(memory_space=pl.ANY)
        vector = pl.BlockSpec(memory_space=pltpu.VMEM)
        out, share = pl.pallas_call(
            functools.partial(kernel, n_tile, n_spec, 3, GROUPS),
            out_shape=(pltpu.VMEM((total, cells), BF16), pltpu.VMEM((1, 1), F32)),
            in_specs=[anywhere] * 7,
            out_specs=(vector, vector),
            scratch_shapes=[
                pltpu.VMEM((halves, species * deep, BLK), F32),
                pltpu.VMEM((halves, deep, BLK), F32),
                pltpu.VMEM((halves, deep, BLK), F32),
                pltpu.VMEM((2, halves, species * 4, BLK), F32),
                pltpu.VMEM((2, halves, species * 4, BLK), F32),
                pltpu.VMEM((2, halves, PAD, BLK), F32),
                pltpu.VMEM((n_spec, GROUPS, species, span), BF16),
                pltpu.VMEM((GROUPS, n_spec, species, span), BF16),
                pltpu.VMEM((total, hidden), BF16),
                pltpu.VMEM((hidden, hidden), BF16),
                pltpu.VMEM((hidden, total), BF16),
                pltpu.VMEM((hidden, hidden), BF16),
                pltpu.VMEM((total, hidden), BF16),
                pltpu.VMEM((5, 8, BLK), jnp.int32),
                pltpu.VMEM((4, 8, BLK), jnp.int32),
                pltpu.SMEM((active.size,), jnp.int32),
                pltpu.SMEM((dest.size,), jnp.int32),
                pltpu.SemaphoreType.DMA((2 * halves,)),
                pltpu.SemaphoreType.DMA((5,)),
                pltpu.SemaphoreType.DMA((4 * halves,)),
                pltpu.SemaphoreType.DMA((4 * halves,)),
                pltpu.SemaphoreType.DMA((4,)),
                pltpu.SemaphoreType.DMA((4,)),
                pltpu.SemaphoreType.DMA,
                pltpu.SemaphoreType.DMA((GROUPS,)),
                pltpu.SemaphoreType.DMA,
                pltpu.SemaphoreType.REGULAR((max(n_spec // 6, 1), 2)),
            ],
            compiler_params=pltpu.CompilerParams(
                collective_id=0, has_side_effects=True, vmem_limit_bytes=60 * 1024 * 1024
            ),
            name="sweep_exchange_chemistry",
        )(conc, courant, w1, w2, w3.T, active.reshape(-1), dest.reshape(-1))
        return out, share

    in_specs = (
        P("spec", "tile", None),
        P("tile", None),
        P(),
        P(),
        P(),
        P("tile", "spec", None),
        P("tile", "spec", None),
    )
    out_specs = (P(None, ("tile", "spec")), P("tile", "spec"))
    return jax.shard_map(shards, mesh=mesh, in_specs=in_specs, out_specs=out_specs, check_vma=False)
```

```python
import functools

import jax
import jax.numpy as jnp
from jax import lax
from jax.experimental import pallas as pl
from jax.experimental.pallas import tpu as pltpu
from jax.sharding import PartitionSpec as P

BLK = 128
RECV = 8
NBR = 2
GROUPS = 8
PAD = 8
MESH = pl.DeviceIdType.MESH
F32 = jnp.float32
BF16 = jnp.bfloat16


def minmod(left, right):
    return jnp.maximum(jnp.minimum(left, right), 0.0) + jnp.minimum(jnp.maximum(left, right), 0.0)


def fused_silu(half):
    return (half + half * jnp.tanh(half)).astype(BF16)


def chemistry(x, w1_t, w2_t, w3_t):
    one = fused_silu(jnp.dot(w1_t[...], x, preferred_element_type=F32))
    two = fused_silu(jnp.dot(w2_t[...], one, preferred_element_type=F32))
    change = jnp.dot(w3_t[...], two, preferred_element_type=F32)
    return (x.astype(F32) + change).astype(BF16)


def choose(flag, fresh, kept):
    mask = jnp.tile(flag, (fresh.shape[0] // flag.shape[0], 1)) > 0
    return jnp.where(mask, fresh.astype(F32), kept.astype(F32)).astype(BF16)


def kernel(
    n_tile, n_spec, n_z, n_group,
    conc, courant, w1_hbm, w2_hbm, w3_hbm, active_hbm, dest_hbm,
    out, share, w1_t, w2_t, w3_t, flags,
    field, rate, half_rest, field_out, field_in, rate_in, send, recv, w1, w2, counts, counts_in, active, dest,
    load_sem, weight_sem, halo_send, halo_recv, count_send, count_recv, send_sem, recv_sem, own_sem, known,
):
    tile = lax.axis_index("tile")
    me = lax.axis_index("spec")
    my_y, my_z = me // n_z, me % n_z
    n_y = n_spec // n_z
    rows = conc.shape[1]
    deep = rows + 2 * PAD
    share_rows = rows // n_spec
    width = conc.shape[2]
    halves = width // BLK
    per_group = share_rows // n_group
    up, down = (tile + 1) % n_tile, (tile + n_tile - 1) % n_tile

    def partner(k):
        return ((my_y + k) % n_y) * n_z + (my_z + k) % n_z

    barrier = pltpu.get_barrier_semaphore()

    def at(dy, dz):
        return ((my_y + dy + n_y) % n_y) * n_z + (my_z + dz) % n_z

    steps = [1, -1, 2, -2]
    column = list(range(1, n_z))
    for dz in column:
        pl.semaphore_signal(barrier, inc=1, device_id={"spec": at(0, dz)}, device_id_type=MESH)
    for dy in (1, -1):
        pl.semaphore_signal(barrier, inc=1, device_id={"spec": at(dy, 0)}, device_id_type=MESH)
    for step in steps:
        pl.semaphore_signal(barrier, inc=1, device_id={"tile": (tile + step + n_tile) % n_tile}, device_id_type=MESH)

    species = conc.shape[0]

    def load(s, carry):
        for c in range(halves):
            pltpu.make_async_copy(
                conc.at[s, :, pl.ds(c * BLK, BLK)], field.at[c, pl.ds(pl.multiple_of(s * deep + PAD, PAD), rows), :], load_sem.at[c]
            ).start()
        return carry

    lax.fori_loop(0, species, load, 0)
    loads = []
    for c in range(halves):
        loads.append(pltpu.make_async_copy(
            courant.at[:, pl.ds(c * BLK, BLK)], rate.at[c, pl.ds(PAD, rows), :], load_sem.at[halves + c]))
        loads[-1].start()
        whole = field.at[c, pl.ds(0, species * rows), :]
        loads.append(pltpu.make_async_copy(whole, whole, load_sem.at[c]))
    weights = [
        pltpu.make_async_copy(w1_hbm, w1, weight_sem.at[0]),
        pltpu.make_async_copy(w2_hbm, w2, weight_sem.at[1]),
        pltpu.make_async_copy(w3_hbm, w3_t, weight_sem.at[2]),
    ]
    lists = [
        pltpu.make_async_copy(active_hbm, active, weight_sem.at[3]),
        pltpu.make_async_copy(dest_hbm, dest, weight_sem.at[4]),
    ]

    for copy in loads:
        copy.wait()
    for c in range(halves):
        half_rest[c, PAD : PAD + rows] = 0.5 * (1.0 - rate[c, PAD : PAD + rows])

    sides = [(PAD + rows - 4, 4, 4, up), (PAD, PAD + rows, 2, down)]
    def advect(d):
        first = PAD + d * share_rows
        finished = []
        for c in range(halves):
            def value(i):
                return field[c, pl.ds(first + i, species, stride=deep), :]

            def rates(i):
                return rate[c, pl.ds(first + i, 1), :], half_rest[c, pl.ds(first + i, 1), :]

            def flux(i, mid, left, right):
                speed, rest = rates(i)
                return speed * (mid + rest * minmod(left, right))

            before, mid = value(-4), value(-3)
            left = mid - before
            flow, once = None, {}
            done = []
            previous, left2, flow2 = None, None, None
            for i in range(-3, share_rows + 1):
                after = value(i + 1)
                right = after - mid
                now = flux(i, mid, left, right)
                if flow is not None:
                    fresh = mid - now + flow
                    once[i] = fresh
                    if i - 1 in once:
                        right2 = fresh - once[i - 1]
                        if left2 is not None:
                            now2 = flux(i - 1, once[i - 1], left2, right2)
                            if flow2 is not None:
                                done.append(once[i - 1] - now2 + flow2)
                            flow2 = now2
                        left2 = right2
                flow, mid, left = now, after, right
            finished.append(done)
        for r in range(share_rows):
            both = jnp.concatenate([finished[c][r] for c in range(halves)], axis=1)
            spot = (r % per_group) * width
            send[d, r // per_group, :, spot : spot + width] = both.astype(BF16)

    def inside(d):
        return (d != 0) & (d != n_spec - 1)

    def first(dz, carry):
        @pl.when(inside(at(0, dz)))
        def _():
            advect(at(0, dz))
        return carry

    lax.fori_loop(1, n_z, first, 0)

    pl.semaphore_wait(barrier, len(column) + 2 + len(steps))

    def message(d, g):
        return pltpu.make_async_remote_copy(
            send.at[d, g], recv.at[g, me], send_sem, recv_sem.at[g], device_id={"spec": d}, device_id_type=MESH)

    for dz in column:
        @pl.when(inside(at(0, dz)))
        def _(d=at(0, dz)):
            def every(g, carry):
                message(d, g).start()
                return carry

            lax.fori_loop(0, n_group, every, 0)

    for copy in lists + weights:
        copy.start()
    for index, (origin, _, thick, _) in enumerate(sides):
        for c in range(halves):
            for s in range(species):
                field_out[index, c, s * thick : (s + 1) * thick] = field[c, s * deep + origin : s * deep + origin + thick]

    halo = []
    for index, (_, _, thick, device) in enumerate(sides):
        for c in range(halves):
            halo.append(pltpu.make_async_remote_copy(
                field_out.at[index, c, pl.ds(0, species * thick)], field_in.at[index, c, pl.ds(0, species * thick)],
                halo_send.at[2 * c + index], halo_recv.at[2 * c + index], device_id={"tile": device}, device_id_type=MESH))
            halo.append(pltpu.make_async_remote_copy(
                rate.at[c, pl.ds(PAD + (rows - PAD if index == 0 else 0), PAD), :], rate_in.at[index, c],
                halo_send.at[4 + 2 * c + index], halo_recv.at[4 + 2 * c + index], device_id={"tile": device}, device_id_type=MESH))
    for copy in halo:
        copy.start()
    for copy in lists:
        copy.wait()
    named = [jnp.int32(0)] * 5
    for j in range(active.shape[0]):
        home = (dest[j] - tile + n_tile + n_tile // 2) % n_tile - n_tile // 2
        valid = active[j] < out.shape[1] // BLK
        for i, step in enumerate([0] + steps):
            named[i] = named[i] + jnp.where(valid & (home == step), 1, 0)
    for i in range(5):
        counts[i] = jnp.full(counts.shape[1:], named[i], jnp.int32)

    tallies = []
    for i, step in enumerate(steps):
        tallies.append(pltpu.make_async_remote_copy(
            counts.at[i + 1], counts_in.at[i], count_send.at[i], count_recv.at[i],
            device_id={"tile": (tile + step + n_tile) % n_tile}, device_id_type=MESH))
    for copy in tallies:
        copy.start()

    farthest = n_y // 2

    def stage(reach, carry):
        for way, dy in enumerate((1, -1)):
            pl.semaphore_signal(known.at[reach - 1, way], inc=1, device_id={"spec": at(dy, 0)}, device_id_type=MESH)

        def piece(i):
            return at(jnp.where(i < n_z, reach, -reach), i + 1)

        def sweep(i, carry):
            alone = (reach == farthest) & (i == n_z)
            d = jnp.where(alone, me, piece(i))

            @pl.when(inside(d) & ((reach < farthest) | (i <= n_z)))
            def _():
                advect(d)
            return carry

        lax.fori_loop(0, 2 * n_z, sweep, 0)
        for way in range(2):
            pl.semaphore_wait(known.at[reach - 1, way], 1)

        def post(i, carry):
            @pl.when(inside(piece(i)) & ((reach < farthest) | (i < n_z)))
            def _():
                message(piece(i), 0).start()
            return carry

        lax.fori_loop(0, 2 * n_z, post, 0)
        return carry

    lax.fori_loop(1, farthest + 1, stage, 0)

    for copy in halo:
        copy.wait()
    for c in range(halves):
        for index, (_, target, thick, _) in enumerate(sides):
            base = index * (PAD + rows)
            rate[c, base : base + PAD] = rate_in[index, c]
            for s in range(species):
                field[c, s * deep + target : s * deep + target + thick] = field_in[index, c, s * thick : (s + 1) * thick]
            half_rest[c, base : base + PAD] = 0.5 * (1.0 - rate[c, base : base + PAD])

    def edge(e, carry):
        d = e * (n_spec - 1)
        advect(d)

        @pl.when(d != me)
        def _():
            message(d, 0).start()
        return carry

    lax.fori_loop(0, 2, edge, 0)

    def later(i, carry):
        g, k = i // (n_spec - 1), i % (n_spec - 1) + 1
        d = partner(k)

        @pl.when((k % n_y != 0) | (d == 0) | (d == n_spec - 1))
        def _():
            message(d, g).start()
        return carry

    lax.fori_loop(n_spec - 1, n_group * (n_spec - 1), later, 0)

    own = pltpu.make_async_copy(send.at[me], recv.at[:, me], own_sem)
    own.start()

    for copy in weights:
        copy.wait()
    w1_t[...] = (w1[...] * BF16(0.5)).T
    w2_t[...] = (w2[...] * BF16(0.5)).T
    own.wait()

    span = recv.shape[3]
    total = n_spec * species

    def arrived(g):
        pltpu.make_async_remote_copy(
            recv.at[g, pl.ds(0, n_spec - 1)], recv.at[g, pl.ds(0, n_spec - 1)], send_sem, recv_sem.at[g],
            device_id={"spec": me}, device_id_type=MESH).wait_recv()

    def listed(block):
        hits = jnp.int32(0)
        for j in range(active.shape[0]):
            hits = hits + jnp.where(active[j] == block, 1, 0)
        return jnp.full((8, BLK), hits, jnp.int32)

    def integrate(g, carry):
        arrived(g)
        x = recv[g].reshape(total, span)
        fresh = chemistry(x, w1_t, w2_t, w3_t)
        for b in range(span // BLK):
            block = g * (span // BLK) + b
            cols = slice(b * BLK, (b + 1) * BLK)
            out[:, pl.ds(pl.multiple_of(block * BLK, BLK), BLK)] = choose(listed(block), fresh[:, cols], x[:, cols])
        return carry

    lax.fori_loop(0, n_group - 1, integrate, 0)
    for b in range(span // BLK):
        flags[b] = listed((n_group - 1) * (span // BLK) + b)

    for copy in tallies:
        copy.wait()
    tally = counts[0] + counts_in[0] + counts_in[1] + counts_in[2] + counts_in[3]
    share[...] = tally[0:1, 0:1].astype(F32) / RECV

    arrived(n_group - 1)
    out[:, (n_group - 1) * span :] = recv[n_group - 1].reshape(total, span)
    pltpu.make_async_remote_copy(
        recv.at[:, pl.ds(0, n_spec - 1)], recv.at[:, pl.ds(0, n_spec - 1)], send_sem, own_sem,
        device_id={"spec": me}, device_id_type=MESH).wait_send()


def finish(part, w1_t, w2_t, w3_t, flags, out, last, sems):
    total, span = last.shape
    head = part.shape[1] - span
    done = pltpu.make_async_copy(part.at[:, pl.ds(0, head)], out.at[:, pl.ds(0, head)], sems.at[0])
    done.start()
    x = part[:, head:]
    fresh = chemistry(x, w1_t, w2_t, w3_t)
    for b in range(span // BLK):
        cols = slice(b * BLK, (b + 1) * BLK)
        last[:, cols] = choose(flags[b], fresh[:, cols], x[:, cols])
    tail = pltpu.make_async_copy(last, out.at[:, pl.ds(head, span)], sems.at[1])
    tail.start()
    done.wait()
    tail.wait()


def solution(mesh):
    n_tile, n_spec = mesh.shape["tile"], mesh.shape["spec"]

    def shards(conc, courant, w1, w2, w3, active, dest):
        species, rows, width = conc.shape
        hidden = w2.shape[0]
        halves = width // BLK
        total = n_spec * species
        cells = rows // n_spec * width
        span = cells // GROUPS
        deep = rows + 2 * PAD
        anywhere = pl.BlockSpec(memory_space=pl.ANY)
        vector = pl.BlockSpec(memory_space=pltpu.VMEM)
        part, share, *rest = pl.pallas_call(
            functools.partial(kernel, n_tile, n_spec, 3, GROUPS),
            out_shape=(
                pltpu.VMEM((total, cells), BF16),
                pltpu.VMEM((1, 1), F32),
                pltpu.VMEM((hidden, total), BF16),
                pltpu.VMEM((hidden, hidden), BF16),
                pltpu.VMEM((total, hidden), BF16),
                pltpu.VMEM((span // BLK, 8, BLK), jnp.int32),
            ),
            in_specs=[anywhere] * 7,
            out_specs=(vector,) * 6,
            scratch_shapes=[
                pltpu.VMEM((halves, species * deep, BLK), F32),
                pltpu.VMEM((halves, deep, BLK), F32),
                pltpu.VMEM((halves, deep, BLK), F32),
                pltpu.VMEM((2, halves, species * 4, BLK), F32),
                pltpu.VMEM((2, halves, species * 4, BLK), F32),
                pltpu.VMEM((2, halves, PAD, BLK), F32),
                pltpu.VMEM((n_spec, GROUPS, species, span), BF16),
                pltpu.VMEM((GROUPS, n_spec, species, span), BF16),
                pltpu.VMEM((total, hidden), BF16),
                pltpu.VMEM((hidden, hidden), BF16),
                pltpu.VMEM((5, 8, BLK), jnp.int32),
                pltpu.VMEM((4, 8, BLK), jnp.int32),
                pltpu.SMEM((active.size,), jnp.int32),
                pltpu.SMEM((dest.size,), jnp.int32),
                pltpu.SemaphoreType.DMA((2 * halves,)),
                pltpu.SemaphoreType.DMA((5,)),
                pltpu.SemaphoreType.DMA((4 * halves,)),
                pltpu.SemaphoreType.DMA((4 * halves,)),
                pltpu.SemaphoreType.DMA((4,)),
                pltpu.SemaphoreType.DMA((4,)),
                pltpu.SemaphoreType.DMA,
                pltpu.SemaphoreType.DMA((GROUPS,)),
                pltpu.SemaphoreType.DMA,
                pltpu.SemaphoreType.REGULAR((max(n_spec // 6, 1), 2)),
            ],
            compiler_params=pltpu.CompilerParams(
                collective_id=0, has_side_effects=True, vmem_limit_bytes=60 * 1024 * 1024
            ),
            name="sweep_exchange_chemistry",
        )(conc, courant, w1, w2, w3.T, active.reshape(-1), dest.reshape(-1))
        out = pl.pallas_call(
            finish,
            out_shape=jax.ShapeDtypeStruct((total, cells), BF16),
            in_specs=[vector] * 5,
            out_specs=anywhere,
            scratch_shapes=[pltpu.VMEM((total, span), BF16), pltpu.SemaphoreType.DMA((2,))],
            compiler_params=pltpu.CompilerParams(vmem_limit_bytes=24 * 1024 * 1024),
            name="last_group",
        )(*[pltpu.with_memory_space_constraint(a, pltpu.VMEM) for a in (part, *rest)])
        return out, share

    in_specs = (
        P("spec", "tile", None),
        P("tile", None),
        P(),
        P(),
        P(),
        P("tile", "spec", None),
        P("tile", "spec", None),
    )
    out_specs = (P(None, ("tile", "spec")), P("tile", "spec"))
    return jax.shard_map(shards, mesh=mesh, in_specs=in_specs, out_specs=out_specs, check_vma=False)
```

```python
import functools

import jax
import jax.numpy as jnp
from jax import lax
from jax.experimental import pallas as pl
from jax.experimental.pallas import tpu as pltpu
from jax.sharding import PartitionSpec as P

BLK = 128
RECV = 8
NBR = 2
GROUPS = 8
PAD = 8
MESH = pl.DeviceIdType.MESH
F32 = jnp.float32
BF16 = jnp.bfloat16


def minmod(left, right):
    return jnp.maximum(jnp.minimum(left, right), 0.0) + jnp.minimum(jnp.maximum(left, right), 0.0)


def fused_silu(half):
    return (half + half * jnp.tanh(half)).astype(BF16)


def chemistry(x, w1_t, w2_t, w3_t):
    one = fused_silu(jnp.dot(w1_t[...], x, preferred_element_type=F32))
    two = fused_silu(jnp.dot(w2_t[...], one, preferred_element_type=F32))
    change = jnp.dot(w3_t[...], two, preferred_element_type=F32)
    return (x.astype(F32) + change).astype(BF16)


def choose(flag, fresh, kept):
    mask = jnp.tile(flag, (fresh.shape[0] // flag.shape[0], 1)) > 0
    return jnp.where(mask, fresh.astype(F32), kept.astype(F32)).astype(BF16)


def kernel(
    n_tile, n_spec, n_z, n_group,
    conc, courant, w1_hbm, w2_hbm, w3_hbm, active_hbm, dest_hbm,
    out, share, w1_t, w2_t, w3_t, flags,
    field, rate, half_rest, field_out, field_in, rate_in, send, recv, w1, w2, counts, counts_in, active, dest,
    load_sem, weight_sem, halo_send, halo_recv, count_send, count_recv, send_sem, recv_sem, own_sem, known,
):
    tile = lax.axis_index("tile")
    me = lax.axis_index("spec")
    my_y, my_z = me // n_z, me % n_z
    n_y = n_spec // n_z
    rows = conc.shape[1]
    deep = rows + 2 * PAD
    share_rows = rows // n_spec
    width = conc.shape[2]
    halves = width // BLK
    per_group = share_rows // n_group
    up, down = (tile + 1) % n_tile, (tile + n_tile - 1) % n_tile

    def partner(k):
        return ((my_y + k) % n_y) * n_z + (my_z + k) % n_z

    barrier = pltpu.get_barrier_semaphore()

    def at(dy, dz):
        return ((my_y + dy + n_y) % n_y) * n_z + (my_z + dz) % n_z

    steps = [1, -1, 2, -2]
    column = list(range(1, n_z))
    for dz in column:
        pl.semaphore_signal(barrier, inc=1, device_id={"spec": at(0, dz)}, device_id_type=MESH)
    for dy in (1, -1):
        pl.semaphore_signal(barrier, inc=1, device_id={"spec": at(dy, 0)}, device_id_type=MESH)
    for step in steps:
        pl.semaphore_signal(barrier, inc=1, device_id={"tile": (tile + step + n_tile) % n_tile}, device_id_type=MESH)

    species = conc.shape[0]

    def load(s, carry):
        for c in range(halves):
            pltpu.make_async_copy(
                conc.at[s, :, pl.ds(c * BLK, BLK)], field.at[c, pl.ds(pl.multiple_of(s * deep + PAD, PAD), rows), :], load_sem.at[c]
            ).start()
        return carry

    lax.fori_loop(0, species, load, 0)
    loads = []
    for c in range(halves):
        loads.append(pltpu.make_async_copy(
            courant.at[:, pl.ds(c * BLK, BLK)], rate.at[c, pl.ds(PAD, rows), :], load_sem.at[halves + c]))
        loads[-1].start()
        whole = field.at[c, pl.ds(0, species * rows), :]
        loads.append(pltpu.make_async_copy(whole, whole, load_sem.at[c]))
    weights = [
        pltpu.make_async_copy(w1_hbm, w1, weight_sem.at[0]),
        pltpu.make_async_copy(w2_hbm, w2, weight_sem.at[1]),
        pltpu.make_async_copy(w3_hbm, w3_t, weight_sem.at[2]),
    ]
    lists = [
        pltpu.make_async_copy(active_hbm, active, weight_sem.at[3]),
        pltpu.make_async_copy(dest_hbm, dest, weight_sem.at[4]),
    ]

    for copy in loads:
        copy.wait()
    for c in range(halves):
        half_rest[c, PAD : PAD + rows] = 0.5 * (1.0 - rate[c, PAD : PAD + rows])

    sides = [(PAD + rows - 4, 4, 4, up), (PAD, PAD + rows, 2, down)]
    def advect(d):
        first = PAD + d * share_rows
        finished = []
        for c in range(halves):
            def value(i):
                return field[c, pl.ds(first + i, species, stride=deep), :]

            def rates(i):
                return rate[c, pl.ds(first + i, 1), :], half_rest[c, pl.ds(first + i, 1), :]

            def flux(i, mid, left, right):
                speed, rest = rates(i)
                return speed * (mid + rest * minmod(left, right))

            before, mid = value(-4), value(-3)
            left = mid - before
            flow, once = None, {}
            done = []
            previous, left2, flow2 = None, None, None
            for i in range(-3, share_rows + 1):
                after = value(i + 1)
                right = after - mid
                now = flux(i, mid, left, right)
                if flow is not None:
                    fresh = mid - now + flow
                    once[i] = fresh
                    if i - 1 in once:
                        right2 = fresh - once[i - 1]
                        if left2 is not None:
                            now2 = flux(i - 1, once[i - 1], left2, right2)
                            if flow2 is not None:
                                done.append(once[i - 1] - now2 + flow2)
                            flow2 = now2
                        left2 = right2
                flow, mid, left = now, after, right
            finished.append(done)
        for r in range(share_rows):
            both = jnp.concatenate([finished[c][r] for c in range(halves)], axis=1)
            spot = (r % per_group) * width
            send[d, r // per_group, :, spot : spot + width] = both.astype(BF16)

    def inside(d):
        return (d != 0) & (d != n_spec - 1)

    def first(dz, carry):
        @pl.when(inside(at(0, dz)))
        def _():
            advect(at(0, dz))
        return carry

    lax.fori_loop(1, n_z, first, 0)

    pl.semaphore_wait(barrier, len(column) + 2 + len(steps))

    def message(d, g):
        return pltpu.make_async_remote_copy(
            send.at[d, g], recv.at[g, me], send_sem, recv_sem.at[g], device_id={"spec": d}, device_id_type=MESH)

    for dz in column:
        @pl.when(inside(at(0, dz)))
        def _(d=at(0, dz)):
            def every(g, carry):
                message(d, g).start()
                return carry

            lax.fori_loop(0, n_group, every, 0)

    for copy in lists + weights:
        copy.start()
    for index, (origin, _, thick, _) in enumerate(sides):
        for c in range(halves):
            for s in range(species):
                field_out[index, c, s * thick : (s + 1) * thick] = field[c, s * deep + origin : s * deep + origin + thick]

    halo = []
    for index, (_, _, thick, device) in enumerate(sides):
        for c in range(halves):
            halo.append(pltpu.make_async_remote_copy(
                field_out.at[index, c, pl.ds(0, species * thick)], field_in.at[index, c, pl.ds(0, species * thick)],
                halo_send.at[2 * c + index], halo_recv.at[2 * c + index], device_id={"tile": device}, device_id_type=MESH))
            halo.append(pltpu.make_async_remote_copy(
                rate.at[c, pl.ds(PAD + (rows - PAD if index == 0 else 0), PAD), :], rate_in.at[index, c],
                halo_send.at[4 + 2 * c + index], halo_recv.at[4 + 2 * c + index], device_id={"tile": device}, device_id_type=MESH))
    for copy in halo:
        copy.start()
    for copy in lists:
        copy.wait()
    named = [jnp.int32(0)] * 5
    for j in range(active.shape[0]):
        home = (dest[j] - tile + n_tile + n_tile // 2) % n_tile - n_tile // 2
        valid = active[j] < out.shape[1] // BLK
        for i, step in enumerate([0] + steps):
            named[i] = named[i] + jnp.where(valid & (home == step), 1, 0)
    for i in range(5):
        counts[i] = jnp.full(counts.shape[1:], named[i], jnp.int32)

    tallies = []
    for i, step in enumerate(steps):
        tallies.append(pltpu.make_async_remote_copy(
            counts.at[i + 1], counts_in.at[i], count_send.at[i], count_recv.at[i],
            device_id={"tile": (tile + step + n_tile) % n_tile}, device_id_type=MESH))
    for copy in tallies:
        copy.start()

    farthest = n_y // 2

    def stage(reach, carry):
        for way, dy in enumerate((1, -1)):
            pl.semaphore_signal(known.at[reach - 1, way], inc=1, device_id={"spec": at(dy, 0)}, device_id_type=MESH)

        def piece(i):
            return at(jnp.where(i < n_z, reach, -reach), i + 1)

        def sweep(i, carry):
            alone = (reach == farthest) & (i == n_z)
            d = jnp.where(alone, me, piece(i))

            @pl.when(inside(d) & ((reach < farthest) | (i <= n_z)))
            def _():
                advect(d)
            return carry

        lax.fori_loop(0, 2 * n_z, sweep, 0)
        for way in range(2):
            pl.semaphore_wait(known.at[reach - 1, way], 1)

        def post(i, carry):
            @pl.when(inside(piece(i)) & ((reach < farthest) | (i < n_z)))
            def _():
                message(piece(i), 0).start()
            return carry

        lax.fori_loop(0, 2 * n_z, post, 0)
        return carry

    lax.fori_loop(1, farthest + 1, stage, 0)

    for copy in halo:
        copy.wait()
    for c in range(halves):
        for index, (_, target, thick, _) in enumerate(sides):
            base = index * (PAD + rows)
            rate[c, base : base + PAD] = rate_in[index, c]
            for s in range(species):
                field[c, s * deep + target : s * deep + target + thick] = field_in[index, c, s * thick : (s + 1) * thick]
            half_rest[c, base : base + PAD] = 0.5 * (1.0 - rate[c, base : base + PAD])

    def edge(e, carry):
        d = e * (n_spec - 1)
        advect(d)

        @pl.when(d != me)
        def _():
            message(d, 0).start()
        return carry

    lax.fori_loop(0, 2, edge, 0)

    def later(i, carry):
        g, at_step = i // (n_spec - 1), i % (n_spec - 1)
        crossing = n_spec - n_y
        k = jnp.where(at_step < crossing, at_step + at_step // (n_z - 1) + 1, n_z * (at_step - crossing + 1))
        d = partner(k)

        @pl.when((k % n_y != 0) | (d == 0) | (d == n_spec - 1))
        def _():
            message(d, g).start()
        return carry

    lax.fori_loop(n_spec - 1, n_group * (n_spec - 1), later, 0)

    own = pltpu.make_async_copy(send.at[me], recv.at[:, me], own_sem)
    own.start()

    for copy in weights:
        copy.wait()
    w1_t[...] = (w1[...] * BF16(0.5)).T
    w2_t[...] = (w2[...] * BF16(0.5)).T
    own.wait()

    span = recv.shape[3]
    total = n_spec * species

    def arrived(g):
        pltpu.make_async_remote_copy(
            recv.at[g, pl.ds(0, n_spec - 1)], recv.at[g, pl.ds(0, n_spec - 1)], send_sem, recv_sem.at[g],
            device_id={"spec": me}, device_id_type=MESH).wait_recv()

    def listed(block):
        hits = jnp.int32(0)
        for j in range(active.shape[0]):
            hits = hits + jnp.where(active[j] == block, 1, 0)
        return jnp.full((8, BLK), hits, jnp.int32)

    def integrate(g, carry):
        arrived(g)
        x = recv[g].reshape(total, span)
        fresh = chemistry(x, w1_t, w2_t, w3_t)
        for b in range(span // BLK):
            block = g * (span // BLK) + b
            cols = slice(b * BLK, (b + 1) * BLK)
            out[:, pl.ds(pl.multiple_of(block * BLK, BLK), BLK)] = choose(listed(block), fresh[:, cols], x[:, cols])
        return carry

    lax.fori_loop(0, n_group - 1, integrate, 0)
    for b in range(span // BLK):
        flags[b] = listed((n_group - 1) * (span // BLK) + b)

    for copy in tallies:
        copy.wait()
    tally = counts[0] + counts_in[0] + counts_in[1] + counts_in[2] + counts_in[3]
    share[...] = tally[0:1, 0:1].astype(F32) / RECV

    arrived(n_group - 1)
    out[:, (n_group - 1) * span :] = recv[n_group - 1].reshape(total, span)
    pltpu.make_async_remote_copy(
        recv.at[:, pl.ds(0, n_spec - 1)], recv.at[:, pl.ds(0, n_spec - 1)], send_sem, own_sem,
        device_id={"spec": me}, device_id_type=MESH).wait_send()


def finish(part, w1_t, w2_t, w3_t, flags, out, last, sems):
    total, span = last.shape
    head = part.shape[1] - span
    done = pltpu.make_async_copy(part.at[:, pl.ds(0, head)], out.at[:, pl.ds(0, head)], sems.at[0])
    done.start()
    x = part[:, head:]
    fresh = chemistry(x, w1_t, w2_t, w3_t)
    for b in range(span // BLK):
        cols = slice(b * BLK, (b + 1) * BLK)
        last[:, cols] = choose(flags[b], fresh[:, cols], x[:, cols])
    tail = pltpu.make_async_copy(last, out.at[:, pl.ds(head, span)], sems.at[1])
    tail.start()
    done.wait()
    tail.wait()


def solution(mesh):
    n_tile, n_spec = mesh.shape["tile"], mesh.shape["spec"]

    def shards(conc, courant, w1, w2, w3, active, dest):
        species, rows, width = conc.shape
        hidden = w2.shape[0]
        halves = width // BLK
        total = n_spec * species
        cells = rows // n_spec * width
        span = cells // GROUPS
        deep = rows + 2 * PAD
        anywhere = pl.BlockSpec(memory_space=pl.ANY)
        vector = pl.BlockSpec(memory_space=pltpu.VMEM)
        part, share, *rest = pl.pallas_call(
            functools.partial(kernel, n_tile, n_spec, 3, GROUPS),
            out_shape=(
                pltpu.VMEM((total, cells), BF16),
                pltpu.VMEM((1, 1), F32),
                pltpu.VMEM((hidden, total), BF16),
                pltpu.VMEM((hidden, hidden), BF16),
                pltpu.VMEM((total, hidden), BF16),
                pltpu.VMEM((span // BLK, 8, BLK), jnp.int32),
            ),
            in_specs=[anywhere] * 7,
            out_specs=(vector,) * 6,
            scratch_shapes=[
                pltpu.VMEM((halves, species * deep, BLK), F32),
                pltpu.VMEM((halves, deep, BLK), F32),
                pltpu.VMEM((halves, deep, BLK), F32),
                pltpu.VMEM((2, halves, species * 4, BLK), F32),
                pltpu.VMEM((2, halves, species * 4, BLK), F32),
                pltpu.VMEM((2, halves, PAD, BLK), F32),
                pltpu.VMEM((n_spec, GROUPS, species, span), BF16),
                pltpu.VMEM((GROUPS, n_spec, species, span), BF16),
                pltpu.VMEM((total, hidden), BF16),
                pltpu.VMEM((hidden, hidden), BF16),
                pltpu.VMEM((5, 8, BLK), jnp.int32),
                pltpu.VMEM((4, 8, BLK), jnp.int32),
                pltpu.SMEM((active.size,), jnp.int32),
                pltpu.SMEM((dest.size,), jnp.int32),
                pltpu.SemaphoreType.DMA((2 * halves,)),
                pltpu.SemaphoreType.DMA((5,)),
                pltpu.SemaphoreType.DMA((4 * halves,)),
                pltpu.SemaphoreType.DMA((4 * halves,)),
                pltpu.SemaphoreType.DMA((4,)),
                pltpu.SemaphoreType.DMA((4,)),
                pltpu.SemaphoreType.DMA,
                pltpu.SemaphoreType.DMA((GROUPS,)),
                pltpu.SemaphoreType.DMA,
                pltpu.SemaphoreType.REGULAR((max(n_spec // 6, 1), 2)),
            ],
            compiler_params=pltpu.CompilerParams(
                collective_id=0, has_side_effects=True, vmem_limit_bytes=60 * 1024 * 1024
            ),
            name="sweep_exchange_chemistry",
        )(conc, courant, w1, w2, w3.T, active.reshape(-1), dest.reshape(-1))
        out = pl.pallas_call(
            finish,
            out_shape=jax.ShapeDtypeStruct((total, cells), BF16),
            in_specs=[vector] * 5,
            out_specs=anywhere,
            scratch_shapes=[pltpu.VMEM((total, span), BF16), pltpu.SemaphoreType.DMA((2,))],
            compiler_params=pltpu.CompilerParams(vmem_limit_bytes=24 * 1024 * 1024),
            name="last_group",
        )(*[pltpu.with_memory_space_constraint(a, pltpu.VMEM) for a in (part, *rest)])
        return out, share

    in_specs = (
        P("spec", "tile", None),
        P("tile", None),
        P(),
        P(),
        P(),
        P("tile", "spec", None),
        P("tile", "spec", None),
    )
    out_specs = (P(None, ("tile", "spec")), P("tile", "spec"))
    return jax.shard_map(shards, mesh=mesh, in_specs=in_specs, out_specs=out_specs, check_vma=False)
```
